32 devices in a mesh: fsdp: 4 (over y, x), req: 8 (over z, core).
Axes of the slice: x: 2, y: 2, z: 4, core: 2. Of those that a mesh axis runs over, the one named last changes fastest.
Arguments:
- x_prompt: bfloat16 [8, 256, 2048], P('req', 'fsdp')
- x_suffix: bfloat16 [8, 4, 256, 2048], P('req', 'fsdp')
- norm_gain: float32 [2048], replicated, may hold values from 0.1 to 1.9
- w_query: bfloat16 [2048, 1024], P('fsdp', 'req')
- w_key: bfloat16 [2048, 512], P('fsdp', 'req')
- w_value: bfloat16 [2048, 512], P('fsdp', 'req'), may hold values from -0.125 to 0.125
- query_gain: float32 [128], replicated
- key_gain: float32 [128], replicated
- adapter_down: bfloat16 [8, 16, 2048], P('fsdp'), may hold values from -0.125 to 0.125
- adapter_up: bfloat16 [8, 16, 1024], P('fsdp'), may hold values from -1.5 to 1.5
- prompt_len: int32 [8], P('req'), may hold values from 64 to 256, as said below
- member_count: int32 [8], P('req'), may hold values from 2 to 4, as said below
- suffix_len: int32 [8, 4], P('req', 'fsdp'), may hold values from 128 to 256, as said below
- adapter_id: int32 [8, 4], P('req'), may hold values from 0 to 7
- holder_slot: int32 [8], replicated, may hold values from 0 to 7, each once
Outputs:
- prompt_out: bfloat16 [8, 256, 1024], P('req', 'fsdp')
- suffix_out: bfloat16 [8, 4, 256, 1024], P('req', 'fsdp')
The draws below stay inside these ranges and needn't reach their ends.
Inputs may be any that keep to these rules, and one draw needn't show every extreme that they name: `prompt_len`: some group's prompt has exactly 256 positions. `member_count`: some group is full. `suffix_len`: some member's suffix has exactly 256 tokens. `holder_slot`: each adapter has its own storage row.
All inputs are finite; a program needn't handle non-finite values.
Results may differ from the reference program's by a relative error of at most 0.0055.
The reference program's roundings to bfloat16 on the way count: a program that leaves them out, or rounds other values in their place, can miss the bound.
Values may be sent and summed in bfloat16 or wider, within the bound.
No kernel may reach another device: no remote copies, remote signals or barrier semaphores. Data moves between devices by JAX's collectives and lax.ppermute only.
A program may use at most 64 MiB of HBM per device.

```python
import jax
import jax.numpy as jnp
from jax import lax

D = 2048
HQ = 8
KVH = 4
HD = 128
RANK = 16
SUF = 256
GROUPS = 8
MEMBERS = 4
PROMPT = 256
ADAPTERS = 8


def draw_gain_values(key):
    return jnp.exp(jax.random.uniform(key, (HD,), jnp.float32, jnp.log(0.8), jnp.log(3.0)))


def draw_query_gain(key, part):
    return draw_gain_values(jax.random.fold_in(key, 11))


def draw_key_gain(key, part):
    return draw_gain_values(jax.random.fold_in(key, 12))


def query_matrix(key):
    return jax.random.normal(jax.random.fold_in(key, 31), (D, HQ * HD), jnp.float32) * D ** (-0.5)


def draw_w_query(key, part):
    return query_matrix(key).astype(jnp.bfloat16)


def draw_w_key(key, part):
    fresh = jax.random.normal(jax.random.fold_in(key, 32), (D, KVH * HD), jnp.float32) * D ** (-0.5)
    return fresh.astype(jnp.bfloat16)


def fresh_rows(key, full_shape):
    source = jax.random.truncated_normal(jax.random.fold_in(key, 1), -6.0, 6.0, full_shape, jnp.float32)
    return source


def draw_x_prompt(key, part):
    return fresh_rows(jax.random.fold_in(key, 41), (GROUPS, PROMPT, D)).astype(jnp.bfloat16)


def draw_x_suffix(key, part):
    return fresh_rows(jax.random.fold_in(key, 42), (GROUPS, MEMBERS, SUF, D)).astype(jnp.bfloat16)


def with_peak(key, full_shape, lowest, highest):
    first_key, second_key = jax.random.split(key)
    drawn = jax.random.randint(first_key, full_shape, lowest, highest + 1)
    cells = 1
    for extent in full_shape:
        cells = cells * extent
    chosen = jax.random.randint(second_key, (), 0, cells)
    flat_index = jnp.arange(cells).reshape(full_shape)
    return jnp.where(flat_index == chosen, highest, drawn).astype(jnp.int32)


def draw_prompt_len(key, part):
    return with_peak(jax.random.fold_in(key, 21), (GROUPS,), PROMPT // 4, PROMPT)


def draw_member_count(key, part):
    return with_peak(jax.random.fold_in(key, 22), (GROUPS,), MEMBERS // 2, MEMBERS)


def draw_suffix_len(key, part):
    return with_peak(jax.random.fold_in(key, 23), (GROUPS, MEMBERS), SUF // 2, SUF)


def set_ends(values, key, smallest, top_value):
    shape = values.shape
    spot = [jax.random.randint(jax.random.fold_in(key, axis), (), 0, shape[axis]) for axis in range(len(shape))]
    values = values.at[tuple(spot)].set(smallest)
    longest = shape.index(max(shape))
    spot[longest] = (spot[longest] + 1) % shape[longest]
    return values.at[tuple(spot)].set(top_value)


def block_scale(own_key, dims, cuts, smallest, top_value):
    gain = 1.0
    for dim, parts in cuts:
        steps = jax.random.uniform(jax.random.fold_in(jax.random.fold_in(own_key, 6), dim), (parts,), jnp.float32, smallest / len(cuts), top_value / len(cuts))
        gain = gain * jnp.repeat(jnp.exp(steps), dims[dim] // parts).reshape((-1,) + (1,) * (len(dims) - 1 - dim))
    return gain


def scatter_about(stream_key, shape, deviation, bound, shards=(), held_as=jnp.bfloat16):
    array = jax.random.normal(stream_key, shape, jnp.float32) * deviation
    if len(shards) > 0:
        array = block_scale(stream_key, shape, shards, -0.22, 0.18) * array
    return jnp.clip(array, min=-bound, max=bound).astype(held_as)


def setup_inputs(seed: int = 0) -> dict:
    splits = jax.random.split(jax.random.key(seed), 16)
    x_prompt = draw_x_prompt(jax.random.fold_in(splits[15], 71), 0)
    x_suffix = draw_x_suffix(jax.random.fold_in(splits[15], 71), 0)
    norm_gain = jnp.clip(1.0 + 0.18 * jax.random.normal(splits[2], (D,), jnp.float32), 0.1, 1.9)
    w_query = draw_w_query(jax.random.fold_in(splits[15], 71), 0)
    w_key = draw_w_key(jax.random.fold_in(splits[15], 71), 0)
    w_value = scatter_about(splits[5], (D, KVH * HD), D ** -0.5, 0.125, ((0, 4), (1, 8)))
    query_gain = draw_query_gain(jax.random.fold_in(splits[15], 71), 0)
    key_gain = draw_key_gain(jax.random.fold_in(splits[15], 71), 0)
    adapter_down = scatter_about(splits[8], (ADAPTERS, RANK, D), D ** -0.5, 0.125, ((0, 4),))
    adapter_up = scatter_about(splits[9], (ADAPTERS, RANK, HQ * HD), RANK ** -0.5, 1.5, ((0, 4),))
    prompt_len = draw_prompt_len(jax.random.fold_in(splits[15], 71), 0)
    member_count = draw_member_count(jax.random.fold_in(splits[15], 71), 0)
    suffix_len = draw_suffix_len(jax.random.fold_in(splits[15], 71), 0)
    adapter_id = set_ends(jax.random.randint(splits[13], (GROUPS, MEMBERS), 0, ADAPTERS), jax.random.fold_in(splits[13], 1), 0, ADAPTERS - 1).astype(jnp.int32)
    holder_slot = jax.random.permutation(splits[14], ADAPTERS).astype(jnp.int32)
    return {"x_prompt": x_prompt, "x_suffix": x_suffix, "norm_gain": norm_gain, "w_query": w_query, "w_key": w_key, "w_value": w_value, "query_gain": query_gain, "key_gain": key_gain, "adapter_down": adapter_down, "adapter_up": adapter_up, "prompt_len": prompt_len, "member_count": member_count, "suffix_len": suffix_len, "adapter_id": adapter_id, "holder_slot": holder_slot}


epsilon = 1e-06
rope_base = 1000000.0
masked_low = -1e+30

def norm_rows(values, gain_vector):
    return values * lax.rsqrt(lax.optimization_barrier(jnp.mean(values * values, axis=-1, keepdims=True)) + epsilon) * gain_vector

def rotate(heads_in, positions):
    half_dim = heads_in.shape[-1] // 2
    frequency = rope_base ** (-jnp.arange(half_dim).astype(jnp.float32) / half_dim)
    angles = positions.astype(jnp.float32)[:, None] * frequency[None, :]
    cosine = jnp.cos(angles)[:, None, :]
    sine = jnp.sin(angles)[:, None, :]
    first_half = heads_in[..., :half_dim]
    second_half = heads_in[..., half_dim:]
    return jnp.concatenate([first_half * cosine - second_half * sine, second_half * cosine + first_half * sine], axis=-1)

def shape_heads(flat_rows, gain_vector, positions, head_dim):
    per_head = flat_rows.reshape(flat_rows.shape[0], flat_rows.shape[1] // head_dim, head_dim)
    return rotate(norm_rows(per_head, gain_vector), positions)

def cast_to_bfloat16(values):
    return lax.optimization_barrier(values.astype(jnp.bfloat16)).astype(jnp.float32)

def attend(queries, key_heads, value_heads, allowed, score_scale):
    scores = jnp.einsum('nkgd,mkd->nkgm', queries, key_heads, precision=lax.Precision.HIGHEST) * score_scale
    visible = allowed[:, None, None, :]
    row_top = lax.optimization_barrier(jnp.max(jnp.where(visible, scores, masked_low), axis=-1, keepdims=True))
    exponent = jnp.where(visible, jnp.exp(scores - row_top), 0.0)
    totals = lax.optimization_barrier(jnp.sum(exponent, axis=-1))
    numerator = jnp.einsum('nkgm,mkd->nkgd', cast_to_bfloat16(exponent), value_heads, precision=lax.Precision.HIGHEST)
    return numerator / totals[..., None]

def reference(x_prompt, x_suffix, norm_gain, w_query, w_key, w_value, query_gain, key_gain, adapter_down, adapter_up, prompt_len, member_count, suffix_len, adapter_id, holder_slot):
    slot_table = jnp.take(holder_slot, adapter_id, axis=0)
    score_scale = HD ** (-0.5)
    group_size = HQ // KVH
    row_count = PROMPT + MEMBERS * SUF

    def one_group(inputs):
        prompt_in, suffix_rows, prompt_total, member_total, suffix_total, slot_row = inputs
        flat_rows = jnp.concatenate([prompt_in, suffix_rows.reshape(MEMBERS * SUF, D)], axis=0)
        normed = norm_rows(flat_rows.astype(jnp.float32), norm_gain).astype(jnp.bfloat16)
        base_q = jnp.dot(normed, w_query, preferred_element_type=jnp.float32)
        base_k = jnp.dot(normed, w_key, preferred_element_type=jnp.float32)
        base_v = jnp.dot(normed, w_value, preferred_element_type=jnp.float32)
        suffix_input_rows = normed[PROMPT:].reshape(MEMBERS, SUF, D).astype(jnp.float32)
        select_down_matrix = jnp.take(adapter_down, slot_row, axis=0).astype(jnp.float32)
        select_up_matrix = jnp.take(adapter_up, slot_row, axis=0).astype(jnp.float32)
        reduced_rank_rows = jnp.einsum('bve,bfe->bvf', suffix_input_rows, select_down_matrix, precision=lax.Precision.HIGHEST)
        adapter_delta = jnp.einsum('wge,wet->wgt', cast_to_bfloat16(reduced_rank_rows), select_up_matrix, precision=lax.Precision.HIGHEST)
        query_full = jnp.concatenate([base_q[:PROMPT], base_q[PROMPT:] + adapter_delta.reshape(MEMBERS * SUF, HQ * HD)], axis=0)
        prompt_pos = jnp.arange(PROMPT).astype(jnp.int32)
        suffix_pos = prompt_total + jnp.tile(jnp.arange(SUF).astype(jnp.int32), MEMBERS)
        positions = jnp.concatenate([prompt_pos, suffix_pos])
        queries = cast_to_bfloat16(shape_heads(query_full, query_gain, positions, HD)).reshape(row_count, KVH, group_size, HD)
        key_heads = cast_to_bfloat16(shape_heads(base_k, key_gain, positions, HD))
        value_heads = cast_to_bfloat16(base_v).reshape(row_count, KVH, HD)
        prompt_k = key_heads[:PROMPT]
        prompt_v = value_heads[:PROMPT]
        key_ok = prompt_pos < prompt_total
        prompt_allowed = key_ok[None, :] & (prompt_pos[None, :] <= prompt_pos[:, None])
        prompt_att = attend(queries[:PROMPT], prompt_k, prompt_v, prompt_allowed, score_scale)
        prompt_res = jnp.where(key_ok[:, None], prompt_att.reshape(PROMPT, HQ * HD), 0.0).astype(jnp.bfloat16)
        causal = jnp.arange(SUF)[None, :] <= jnp.arange(SUF)[:, None]
        suffix_allowed = jnp.concatenate([jnp.broadcast_to(key_ok[None, :], (SUF, PROMPT)), causal], axis=1)
        suffix_q = queries[PROMPT:].reshape(MEMBERS, SUF, KVH, group_size, HD)
        suffix_k = key_heads[PROMPT:].reshape(MEMBERS, SUF, KVH, HD)
        suffix_v = value_heads[PROMPT:].reshape(MEMBERS, SUF, KVH, HD)

        def one_member(member):
            member_q, member_k, member_v = member
            return attend(member_q, jnp.concatenate([prompt_k, member_k], axis=0), jnp.concatenate([prompt_v, member_v], axis=0), suffix_allowed, score_scale)
        suffix_att = lax.map(one_member, (suffix_q, suffix_k, suffix_v))
        member_ok = (jnp.arange(MEMBERS) < member_total)[:, None] & (jnp.arange(SUF)[None, :] < suffix_total[:, None])
        suffix_res = jnp.where(member_ok[:, :, None], suffix_att.reshape(MEMBERS, SUF, HQ * HD), 0.0).astype(jnp.bfloat16)
        return (prompt_res, suffix_res)
    prompt_out, suffix_out = lax.map(one_group, (x_prompt, x_suffix, prompt_len, member_count, suffix_len, slot_table))
    return (prompt_out, suffix_out)
```

```python
import functools

import jax
import jax.numpy as jnp
from jax import lax
from jax.experimental import pallas as pl
from jax.experimental.pallas import tpu as pltpu
from jax.sharding import PartitionSpec as P

epsilon = 1e-06
rope_base = 1000000.0
masked_low = -1e30


def norm_rows(values, gain_vector):
    return (
        values
        * lax.rsqrt(jnp.mean(values * values, axis=-1, keepdims=True) + epsilon)
        * gain_vector
    )


def rotate(heads_in, positions):
    half_dim = heads_in.shape[-1] // 2
    frequency = rope_base ** (-jnp.arange(half_dim).astype(jnp.float32) / half_dim)
    angles = positions.astype(jnp.float32)[:, None] * frequency[None, :]
    cosine = jnp.cos(angles)[:, None, :]
    sine = jnp.sin(angles)[:, None, :]
    first_half = heads_in[..., :half_dim]
    second_half = heads_in[..., half_dim:]
    return jnp.concatenate(
        [first_half * cosine - second_half * sine, second_half * cosine + first_half * sine],
        axis=-1,
    )


def shape_heads(flat_rows, gain_vector, positions, head_dim):
    per_head = flat_rows.reshape(flat_rows.shape[0], flat_rows.shape[1] // head_dim, head_dim)
    return rotate(norm_rows(per_head, gain_vector), positions)


def update(carried, scores, allowed, value_heads, pattern):
    running, denominator, summed_output = carried
    masked = jnp.where(allowed, scores, masked_low)
    newest = jnp.maximum(running, jnp.max(masked, axis=-1))
    weights = jnp.where(allowed, jnp.exp(scores - newest[..., None]), 0.0)
    factor = jnp.exp(running - newest)
    denominator = denominator * factor + jnp.sum(weights, axis=-1)
    summed_output = summed_output * factor[..., None] + jnp.einsum(
        pattern, weights.astype(jnp.bfloat16), value_heads, preferred_element_type=jnp.float32
    )
    return (newest, denominator, summed_output)


def shards_general(
    x_prompt,
    x_suffix,
    norm_gain,
    w_query,
    w_key,
    w_value,
    query_gain,
    key_gain,
    adapter_down,
    adapter_up,
    prompt_len,
    member_count,
    suffix_len,
    adapter_id,
    holder_slot,
):
    fsdp_rank = lax.axis_index("fsdp")
    req_count = lax.axis_size("req")
    pr_rows = x_prompt.shape[1]
    mem_dev = x_suffix.shape[1]
    suf_rows = x_suffix.shape[2]
    model_width = x_prompt.shape[2]
    head_dim = query_gain.shape[0]
    q_cols = w_query.shape[1] * req_count
    kv_cols = w_key.shape[1] * req_count
    kv_heads = kv_cols // head_dim
    group_size = q_cols // kv_cols
    row_count = pr_rows + mem_dev * suf_rows
    prompt_total = prompt_len[0]
    tokens = jnp.concatenate(
        [x_prompt[0], x_suffix[0].reshape(mem_dev * suf_rows, model_width)], axis=0
    )
    normed = norm_rows(tokens.astype(jnp.float32), norm_gain).astype(jnp.bfloat16)
    full_q, full_k, full_v = (
        lax.all_gather(w_query, "req", axis=1, tiled=True),
        lax.all_gather(w_key, "req", axis=1, tiled=True),
        lax.all_gather(w_value, "req", axis=1, tiled=True),
    )
    pieces = (
        lax.all_gather(full_q, "fsdp", axis=0, tiled=True),
        lax.all_gather(full_k, "fsdp", axis=0, tiled=True),
        lax.all_gather(full_v, "fsdp", axis=0, tiled=True),
    )
    base_q, base_k, base_v = tuple(
        (
            jnp.dot(normed, weight_piece, preferred_element_type=jnp.float32)
            for weight_piece in pieces
        )
    )
    member_ids = adapter_id[0]
    store_rows = holder_slot.shape[0]
    lookup = jnp.where(
        member_ids[:, None] == jnp.arange(store_rows)[None, :], holder_slot[None, :], 0
    )
    storage = jnp.sum(lookup, axis=1)
    store_down, store_up = (
        lax.all_gather(adapter_down, "fsdp", axis=0, tiled=True),
        lax.all_gather(adapter_up, "fsdp", axis=0, tiled=True),
    )
    mine = lax.dynamic_slice_in_dim(storage, fsdp_rank * mem_dev, mem_dev)
    select_down_matrix = jnp.take(store_down, mine, axis=0)
    select_up_matrix = jnp.take(store_up, mine, axis=0)
    suffix_input_rows = normed[pr_rows:].reshape(mem_dev, suf_rows, model_width)
    reduced_rank_rows = jnp.einsum(
        "bve,bfe->bvf", suffix_input_rows, select_down_matrix, preferred_element_type=jnp.float32
    ).astype(jnp.bfloat16)
    adapter_delta = jnp.einsum(
        "wge,wet->wgt", reduced_rank_rows, select_up_matrix, preferred_element_type=jnp.float32
    )
    query_full = jnp.concatenate(
        [base_q[:pr_rows], base_q[pr_rows:] + adapter_delta.reshape(mem_dev * suf_rows, q_cols)],
        axis=0,
    )
    prompt_pos = fsdp_rank * pr_rows + jnp.arange(pr_rows)
    suffix_pos = prompt_total + jnp.tile(jnp.arange(suf_rows), mem_dev)
    positions = jnp.concatenate([prompt_pos, suffix_pos])
    queries = (
        shape_heads(query_full, query_gain, positions, head_dim)
        .astype(jnp.bfloat16)
        .reshape(row_count, kv_heads, group_size, head_dim)
    )
    key_heads = shape_heads(base_k, key_gain, positions, head_dim).astype(jnp.bfloat16)
    value_heads = base_v.astype(jnp.bfloat16).reshape(row_count, kv_heads, head_dim)
    limits = jnp.concatenate([prompt_pos, jnp.full((mem_dev * suf_rows,), 2**30, jnp.int32)])
    score_scale = head_dim ** (-0.5)
    start_state = (
        jnp.full((row_count, kv_heads, group_size), masked_low, jnp.float32),
        jnp.zeros((row_count, kv_heads, group_size), jnp.float32),
        jnp.zeros((row_count, kv_heads, group_size, head_dim), jnp.float32),
    )
    prompt_k_flat = key_heads[:pr_rows].reshape(pr_rows, kv_cols)
    prompt_v_flat = value_heads[:pr_rows].reshape(pr_rows, kv_cols)
    piece_keys = lax.all_gather(prompt_k_flat, "fsdp", axis=0, tiled=True)
    piece_values = lax.all_gather(prompt_v_flat, "fsdp", axis=0, tiled=True)
    piece_rows = piece_keys.shape[0]
    key_pos = jnp.arange(piece_rows)
    allowed = (key_pos[None, :] < prompt_total) & (key_pos[None, :] <= limits[:, None])
    scores = (
        jnp.einsum(
            "rkgd,nkd->rkgn",
            queries,
            piece_keys.reshape(piece_rows, kv_heads, head_dim),
            preferred_element_type=jnp.float32,
        )
        * score_scale
    )
    carried = update(
        start_state,
        scores,
        allowed[:, None, None, :],
        piece_values.reshape(piece_rows, kv_heads, head_dim),
        "rkgn,nkd->rkgd",
    )
    suffix_state = tuple(
        (
            state_part[pr_rows:].reshape((mem_dev, suf_rows) + state_part.shape[1:])
            for state_part in carried
        )
    )
    suffix_q = queries[pr_rows:].reshape(mem_dev, suf_rows, kv_heads, group_size, head_dim)
    suffix_k = key_heads[pr_rows:].reshape(mem_dev, suf_rows, kv_heads, head_dim)
    suffix_v = value_heads[pr_rows:].reshape(mem_dev, suf_rows, kv_heads, head_dim)
    own_scores = (
        jnp.einsum("mskgd,mtkd->mskgt", suffix_q, suffix_k, preferred_element_type=jnp.float32)
        * score_scale
    )
    causal = jnp.arange(suf_rows)[None, :] <= jnp.arange(suf_rows)[:, None]
    suffix_state = update(
        suffix_state, own_scores, causal[None, :, None, None, :], suffix_v, "mskgt,mtkd->mskgd"
    )
    denominator = jnp.concatenate(
        [carried[1][:pr_rows], suffix_state[1].reshape(mem_dev * suf_rows, kv_heads, group_size)],
        axis=0,
    )
    summed_output = jnp.concatenate(
        [
            carried[2][:pr_rows],
            suffix_state[2].reshape(mem_dev * suf_rows, kv_heads, group_size, head_dim),
        ],
        axis=0,
    )
    attended = (summed_output / denominator[..., None]).reshape(row_count, q_cols)
    member_index = fsdp_rank * mem_dev + jnp.arange(mem_dev)
    suffix_ok = (member_index < member_count[0])[:, None] & (
        jnp.arange(suf_rows)[None, :] < suffix_len[0][:, None]
    )
    valid_rows = jnp.concatenate([prompt_pos < prompt_total, suffix_ok.reshape(mem_dev * suf_rows)])
    result = jnp.where(valid_rows[:, None], attended, 0.0).astype(jnp.bfloat16)
    return (result[:pr_rows][None], result[pr_rows:].reshape(1, mem_dev, suf_rows, q_cols))


axes = ("fsdp", "req")
any_space = pl.BlockSpec(memory_space=pl.ANY)
in_vmem = pl.BlockSpec(memory_space=pltpu.VMEM)
in_smem = pl.BlockSpec(memory_space=pltpu.SMEM)
nt_dims = (((1,), (1,)), ((), ()))


def device_number(x, y, z, core):
    return (y * 2 + x) * 8 + z * 2 + core


def pairs(target):
    return [
        (device_number(x, y, z, core), device_number(*target(x, y, z, core)))
        for y in range(2)
        for x in range(2)
        for z in range(4)
        for core in range(2)
    ]


first_hop = pairs(lambda x, y, z, c: (1 - x, y, z, c) if c == 0 else (x, 1 - y, z, c))
second_hop = pairs(lambda x, y, z, c: (x, 1 - y, z, c) if c == 0 else (1 - x, y, z, c))
ring_hop = pairs(lambda x, y, z, c: (x, y, (z + 1) % 4, c))
core_swap = pairs(lambda x, y, z, c: (x, y, z, 1 - c))
x_swap = pairs(lambda x, y, z, c: (1 - x, y, z, c))
y_swap = pairs(lambda x, y, z, c: (x, 1 - y, z, c))
xy_swap = pairs(lambda x, y, z, c: (1 - x, 1 - y, z, c))


def permute(value, hop):
    return lax.ppermute(value, axes, hop)


def place():
    fsdp_rank = lax.axis_index("fsdp")
    req_rank = lax.axis_index("req")
    return fsdp_rank, lax.rem(fsdp_rank, 2), fsdp_rank // 2, req_rank // 2, lax.rem(req_rank, 2)


def slice_owner(kind, parity):
    rank, x, y, _, _ = place()
    if kind == 0:
        return rank
    x_side = rank + 1 - 2 * x
    y_side = rank + 2 - 4 * y
    if kind == 1:
        return (1 - parity) * x_side + parity * y_side
    if kind == 2:
        return (1 - parity) * y_side + parity * x_side
    return 3 - rank


def pack_kernel(key_ref, value_ref, query_ref, down_ref, up_ref, own_ref, kv_ref, q_ref):
    core = lax.rem(lax.axis_index("req"), 2)
    half = key_ref.shape[0]
    depth = key_ref.shape[1]
    rank = down_ref.shape[1]
    own_ref[0:half, :] = key_ref[...]
    own_ref[half : 2 * half, :] = value_ref[...]
    kv_ref[0:half, :] = key_ref[...]
    kv_ref[half : 2 * half, :] = value_ref[...]
    turned = query_ref[...].T
    own_ref[2 * half : 4 * half, :] = turned
    q_ref[...] = turned
    row = 4 * half
    for source in (down_ref, up_ref):
        for part in range(source.shape[2] // depth):
            own_ref[row : row + rank, :] = source[core, :, part * depth : (part + 1) * depth]
            row += rank


def copy_blocks(sources, parts, sems, target):
    copies = []
    _, _, _, z, core = place()
    for step, (group, row, rows) in enumerate(parts):
        home = lax.rem(z + 4 - step, 4)
        started = []
        for side in range(2):
            parity = core if side == 0 else 1 - core
            for kind in range(4):
                copy = pltpu.make_async_copy(
                    sources[group][side][kind].at[pl.ds(row, rows), :],
                    target(home, parity, slice_owner(kind, parity)),
                    sems.at[step, side * 4 + kind],
                )
                copy.start()
                started.append(copy)
        copies.append((home, started))
    return copies


def project_kv(*refs, rank_size):
    (x_ref, cos_ref, sin_ref, gain_ref, slot_ref), refs = refs[:5], refs[5:]
    own = (refs[0:4], refs[4:8])
    far = (refs[8:12], refs[12:16])
    shared_ref, key_ref, value_ref, low_ref, up_ref, weights, store, sems, store_sems = refs[16:]
    depth = own[0][0].shape[1]
    rows = 128
    pr_rows = shared_ref.shape[0]
    kv_cols = key_ref.shape[1]
    parts = [(0, 0, rows)] + [(1, rows * s, rows) for s in range(3)]

    def target(home, parity, owner):
        return weights.at[
            home,
            pl.ds(pl.multiple_of(parity * rows, rows), rows),
            pl.ds(pl.multiple_of(owner * depth, depth), depth),
        ]

    copies = copy_blocks((own, far), parts, sems, target)
    _, _, _, _, core = place()
    store_copies = []
    for side in range(2):
        parity = core if side == 0 else 1 - core
        for kind in range(4):
            copy = pltpu.make_async_copy(
                own[side][kind].at[pl.ds(2 * rows, store.shape[1]), :],
                store.at[slice_owner(kind, parity) * 2 + parity],
                store_sems.at[side * 4 + kind],
            )
            copy.start()
            store_copies.append(copy)
    cosine = cos_ref[...]
    sine = sin_ref[...]
    low_gain = gain_ref[:, 0:64]
    high_gain = gain_ref[:, 64:128]
    for home, started in copies:
        for copy in started:
            copy.wait()
        both = lax.dot_general(
            x_ref[...], weights[home], nt_dims, preferred_element_type=jnp.float32
        )
        low, high = both[:, 0:64], both[:, 128:192]
        square = jnp.sum(low * low, axis=-1, keepdims=True) + jnp.sum(
            high * high, axis=-1, keepdims=True
        )
        scale = lax.rsqrt(square * (1.0 / 128.0) + epsilon)
        low = low * scale * low_gain
        high = high * scale * high_gain
        keys = jnp.concatenate(
            [low * cosine - high * sine, high * cosine + low * sine], axis=-1
        ).astype(jnp.bfloat16)
        values = jnp.concatenate([both[:, 64:128], both[:, 192:256]], axis=-1).astype(jnp.bfloat16)
        at_head = pl.ds(pl.multiple_of(home * 128, 128), 128)
        shared_ref[:, at_head] = keys[:pr_rows]
        shared_ref[:, pl.ds(pl.multiple_of(home * 128 + kv_cols, 128), 128)] = values[:pr_rows]
        key_ref[:, at_head] = keys[pr_rows:]
        value_ref[:, at_head] = values[pr_rows:]
    for copy in store_copies:
        copy.wait()
    slot = slot_ref[0]
    total = jnp.zeros((x_ref.shape[0] - pr_rows, rank_size), jnp.float32)
    for part in range(x_ref.shape[1] // depth):
        total += lax.dot_general(
            x_ref[pr_rows:, part * depth : (part + 1) * depth],
            store[slot, part * rank_size : (part + 1) * rank_size, :],
            nt_dims,
            preferred_element_type=jnp.float32,
        )
    low_ref[...] = total.astype(jnp.bfloat16)
    row = (x_ref.shape[1] // depth) * rank_size
    for part in range(up_ref.shape[1] // depth):
        up_ref[:, part * depth : (part + 1) * depth] = store[slot, row : row + rank_size, :]
        row += rank_size


def attend_kernel(*refs):
    (x_ref, cos_ref, sin_ref, gain_ref, info_ref, low_ref, up_ref, key_ref, value_ref), refs = (
        refs[:9],
        refs[9:],
    )
    own = (refs[0:4], refs[4:8])
    far = (refs[8:12], refs[12:16])
    shared_parts = refs[16:20]
    prompt_out, suffix_out, weights, shared, sems, shared_sems = refs[20:]
    depth = own[0][0].shape[1]
    rows = 128
    pr_rows = prompt_out.shape[0]
    suf_rows = suffix_out.shape[0]
    row_count = pr_rows + suf_rows
    kv_cols = key_ref.shape[1]
    fsdp_rank, x, y, _, _ = place()
    parts = [(0, rows, rows)] + [(1, rows * s, rows) for s in range(3)]

    def target(home, parity, owner):
        return weights.at[
            home,
            pl.ds(pl.multiple_of(parity * rows, rows), rows),
            pl.ds(pl.multiple_of(owner * depth, depth), depth),
        ]

    copies = copy_blocks((own, far), parts, sems, target)
    owners = (fsdp_rank, fsdp_rank + 1 - 2 * x, fsdp_rank + 2 - 4 * y, 3 - fsdp_rank)
    shared_copies = []
    for index, owner in enumerate(owners):
        copy = pltpu.make_async_copy(
            shared_parts[index],
            shared.at[pl.ds(pl.multiple_of(owner * pr_rows, pr_rows), pr_rows), :],
            shared_sems.at[index],
        )
        copy.start()
        shared_copies.append(copy)
    for copy in shared_copies:
        copy.wait()
    prompt_total = info_ref[0]
    member_ok = info_ref[1]
    suffix_total = info_ref[2]
    prompt_keys = shared.shape[0]
    row = lax.broadcasted_iota(jnp.int32, (row_count, prompt_keys), 0)
    column = lax.broadcasted_iota(jnp.int32, (row_count, prompt_keys), 1)
    limit = jnp.where(row < pr_rows, fsdp_rank * pr_rows + row, jnp.int32(2**30))
    see_prompt = (column < prompt_total) & (column <= limit)
    see_own = lax.broadcasted_iota(jnp.int32, (suf_rows, suf_rows), 1) <= (
        lax.broadcasted_iota(jnp.int32, (suf_rows, suf_rows), 0)
    )
    row = lax.broadcasted_iota(jnp.int32, (row_count, 1), 0)
    prompt_ok = (row < pr_rows) & (fsdp_rank * pr_rows + row < prompt_total)
    suffix_ok = (row >= pr_rows) & (row - pr_rows < suffix_total) & (member_ok > 0)
    row_ok = prompt_ok | suffix_ok
    score_scale = 128 ** (-0.5)
    for home, started in copies:
        for copy in started:
            copy.wait()
        both = lax.dot_general(
            x_ref[...], weights[home], nt_dims, preferred_element_type=jnp.float32
        )
        at_pair = pl.ds(pl.multiple_of(home * 256, 256), 256)
        delta = jnp.dot(low_ref[...], up_ref[:, at_pair], preferred_element_type=jnp.float32)
        both = jnp.concatenate([both[:pr_rows], both[pr_rows:] + delta], axis=0)
        at_head = pl.ds(pl.multiple_of(home * 128, 128), 128)
        p_keys = shared[:, at_head]
        p_values = shared[:, pl.ds(pl.multiple_of(home * 128 + kv_cols, 128), 128)]
        s_keys = key_ref[:, at_head]
        s_values = value_ref[:, at_head]
        for head in range(2):
            query = both[:, head * 128 : head * 128 + 128]
            scale = lax.rsqrt(jnp.mean(query * query, axis=-1, keepdims=True) + epsilon)
            query = query * scale * gain_ref[...]
            query = query * cos_ref[...] + pltpu.roll(query, 64, 1) * sin_ref[...]
            query = query.astype(jnp.bfloat16)
            p_scores = lax.dot_general(
                query, p_keys, nt_dims, preferred_element_type=jnp.float32
            )
            p_scores = jnp.where(see_prompt, p_scores * score_scale, masked_low)
            s_scores = lax.dot_general(
                query[pr_rows:], s_keys, nt_dims, preferred_element_type=jnp.float32
            )
            s_scores = jnp.where(see_own, s_scores * score_scale, masked_low)
            p_top = jnp.max(p_scores, axis=-1, keepdims=True)
            s_top = jnp.max(s_scores, axis=-1, keepdims=True)
            s_top = jnp.maximum(p_top[pr_rows:], s_top)
            top = jnp.concatenate([p_top[:pr_rows], s_top], axis=0)
            p_weights = jnp.exp(p_scores - top)
            s_weights = jnp.exp(s_scores - s_top)
            p_total = jnp.sum(p_weights, axis=-1, keepdims=True)
            s_total = jnp.sum(s_weights, axis=-1, keepdims=True)
            p_sum = jnp.dot(
                p_weights.astype(jnp.bfloat16), p_values, preferred_element_type=jnp.float32
            )
            s_sum = jnp.dot(
                s_weights.astype(jnp.bfloat16), s_values, preferred_element_type=jnp.float32
            )
            p_result = jnp.where(row_ok[:pr_rows], p_sum[:pr_rows] / p_total[:pr_rows], 0.0)
            s_result = (p_sum[pr_rows:] + s_sum) / (p_total[pr_rows:] + s_total)
            s_result = jnp.where(row_ok[pr_rows:], s_result, 0.0)
            at_query = pl.ds(pl.multiple_of(home * 256 + head * 128, 128), 128)
            prompt_out[:, at_query] = p_result.astype(jnp.bfloat16)
            suffix_out[:, at_query] = s_result.astype(jnp.bfloat16)


def spread(block):
    side = permute(block, first_hop)
    other = permute(block, second_hop)
    corner = permute(side, second_hop)
    mine = (block, side, other, corner)
    return mine + tuple(permute(part, core_swap) for part in mine)


def rope_tables(positions, half_dim):
    frequency = rope_base ** (-jnp.arange(half_dim).astype(jnp.float32) / half_dim)
    angles = positions.astype(jnp.float32)[:, None] * frequency[None, :]
    return jnp.cos(angles), jnp.sin(angles)


def shards_torus(
    x_prompt,
    x_suffix,
    norm_gain,
    w_query,
    w_key,
    w_value,
    query_gain,
    key_gain,
    adapter_down,
    adapter_up,
    prompt_len,
    member_count,
    suffix_len,
    adapter_id,
    holder_slot,
):
    bf16 = jnp.bfloat16
    fsdp_rank = lax.axis_index("fsdp")
    pr_rows, model_width = x_prompt.shape[1:]
    suf_rows = x_suffix.shape[2]
    row_count = pr_rows + suf_rows
    depth = w_query.shape[0]
    rank_size = adapter_down.shape[1]
    q_cols = adapter_up.shape[2]
    kv_cols = w_key.shape[1] * 8
    store_rows = (model_width + q_cols) // depth * rank_size

    own, kv_near, q_near = pl.pallas_call(
        pack_kernel,
        out_shape=(
            jax.ShapeDtypeStruct((256 + store_rows, depth), bf16),
            jax.ShapeDtypeStruct((128, depth), bf16),
            jax.ShapeDtypeStruct((128, depth), bf16),
        ),
        name="pack",
    )(w_key.T, w_value.T, w_query, adapter_down, adapter_up)

    def ring(block):
        steps = []
        for _ in range(3):
            block = permute(block, ring_hop)
            steps.append(block)
        return jnp.concatenate(steps, axis=0)

    own_blocks = spread(own)
    kv_blocks = spread(ring(kv_near))
    q_blocks = spread(ring(q_near))

    tokens = jnp.concatenate([x_prompt[0], x_suffix[0, 0]], axis=0)
    normed = norm_rows(tokens.astype(jnp.float32), norm_gain).astype(bf16)
    prompt_pos = fsdp_rank * pr_rows + jnp.arange(pr_rows)
    suffix_pos = prompt_len[0] + jnp.arange(suf_rows)
    cosine, sine = rope_tables(jnp.concatenate([prompt_pos, suffix_pos]), 64)
    lookup = jnp.where(
        adapter_id[0][:, None] == jnp.arange(holder_slot.shape[0])[None, :], holder_slot[None, :], 0
    )
    storage = jnp.sum(lookup, axis=1)
    mine = lax.dynamic_slice_in_dim(storage, fsdp_rank, 1)
    info = jnp.stack(
        [
            prompt_len[0],
            (fsdp_rank < member_count[0]).astype(jnp.int32),
            suffix_len[0, 0],
        ]
    )

    shared, s_keys, s_values, low, up = pl.pallas_call(
        functools.partial(project_kv, rank_size=rank_size),
        out_shape=(
            jax.ShapeDtypeStruct((pr_rows, 2 * kv_cols), bf16),
            jax.ShapeDtypeStruct((suf_rows, kv_cols), bf16),
            jax.ShapeDtypeStruct((suf_rows, kv_cols), bf16),
            jax.ShapeDtypeStruct((suf_rows, rank_size), bf16),
            jax.ShapeDtypeStruct((rank_size, q_cols), bf16),
        ),
        in_specs=[in_vmem] * 4 + [in_smem] + [any_space] * 16,
        scratch_shapes=[
            pltpu.VMEM((4, 256, model_width), bf16),
            pltpu.VMEM((8, store_rows, depth), bf16),
            pltpu.SemaphoreType.DMA((4, 8)),
            pltpu.SemaphoreType.DMA((8,)),
        ],
        compiler_params=pltpu.CompilerParams(vmem_limit_bytes=32 << 20),
        cost_estimate=pl.CostEstimate(
            flops=2 * row_count * model_width * 2 * kv_cols,
            bytes_accessed=8 << 20,
            transcendentals=0,
        ),
        name="project_kv",
    )(normed, cosine, sine, key_gain[None, :], mine, *own_blocks, *kv_blocks)

    shared_blocks = (
        shared,
        permute(shared, x_swap),
        permute(shared, y_swap),
        permute(shared, xy_swap),
    )
    cos_pair = jnp.concatenate([cosine, cosine], axis=1)
    sin_pair = jnp.concatenate([-sine, sine], axis=1)
    prompt_res, suffix_res = pl.pallas_call(
        attend_kernel,
        out_shape=(
            jax.ShapeDtypeStruct((pr_rows, q_cols), bf16),
            jax.ShapeDtypeStruct((suf_rows, q_cols), bf16),
        ),
        in_specs=[in_vmem] * 4 + [in_smem] + [in_vmem] * 4 + [any_space] * 20,
        scratch_shapes=[
            pltpu.VMEM((4, 256, model_width), bf16),
            pltpu.VMEM((4 * pr_rows, 2 * kv_cols), bf16),
            pltpu.SemaphoreType.DMA((4, 8)),
            pltpu.SemaphoreType.DMA((4,)),
        ],
        compiler_params=pltpu.CompilerParams(vmem_limit_bytes=40 << 20),
        cost_estimate=pl.CostEstimate(
            flops=2 * row_count * model_width * q_cols,
            bytes_accessed=8 << 20,
            transcendentals=0,
        ),
        name="attend",
    )(
        normed,
        cos_pair,
        sin_pair,
        query_gain[None, :],
        info,
        low,
        up,
        s_keys,
        s_values,
        *own_blocks,
        *q_blocks,
        *shared_blocks,
    )
    return prompt_res[None], suffix_res[None, None]


def shards(*operands):
    x_suffix, w_query, w_key, query_gain = operands[1], operands[3], operands[4], operands[6]
    head_dim = query_gain.shape[0]
    fits = (
        (lax.axis_size("fsdp"), lax.axis_size("req")) == (4, 8)
        and head_dim == 128
        and w_query.shape[1] == head_dim
        and 2 * w_key.shape[1] == head_dim
        and x_suffix.shape[1] == 1
        and operands[8].shape[0] == 2
    )
    return shards_torus(*operands) if fits else shards_general(*operands)


def solution(mesh):
    return jax.shard_map(
        shards,
        mesh=mesh,
        in_specs=(
            P("req", "fsdp", None),
            P("req", "fsdp", None, None),
            P(),
            P("fsdp", "req"),
            P("fsdp", "req"),
            P("fsdp", "req"),
            P(),
            P(),
            P("fsdp", None, None),
            P("fsdp", None, None),
            P("req"),
            P("req"),
            P("req", "fsdp"),
            P("req", None),
            P(),
        ),
        out_specs=(P("req", "fsdp", None), P("req", "fsdp", None, None)),
        check_vma=False,
    )
```

```python
import functools

import jax
import jax.numpy as jnp
from jax import lax
from jax.experimental import pallas as pl
from jax.experimental.pallas import tpu as pltpu
from jax.sharding import PartitionSpec as P

epsilon = 1e-06
rope_base = 1000000.0
masked_low = -1e30


def norm_rows(values, gain_vector):
    return (
        values
        * lax.rsqrt(jnp.mean(values * values, axis=-1, keepdims=True) + epsilon)
        * gain_vector
    )


def rotate(heads_in, positions):
    half_dim = heads_in.shape[-1] // 2
    frequency = rope_base ** (-jnp.arange(half_dim).astype(jnp.float32) / half_dim)
    angles = positions.astype(jnp.float32)[:, None] * frequency[None, :]
    cosine = jnp.cos(angles)[:, None, :]
    sine = jnp.sin(angles)[:, None, :]
    first_half = heads_in[..., :half_dim]
    second_half = heads_in[..., half_dim:]
    return jnp.concatenate(
        [first_half * cosine - second_half * sine, second_half * cosine + first_half * sine],
        axis=-1,
    )


def shape_heads(flat_rows, gain_vector, positions, head_dim):
    per_head = flat_rows.reshape(flat_rows.shape[0], flat_rows.shape[1] // head_dim, head_dim)
    return rotate(norm_rows(per_head, gain_vector), positions)


def update(carried, scores, allowed, value_heads, pattern):
    running, denominator, summed_output = carried
    masked = jnp.where(allowed, scores, masked_low)
    newest = jnp.maximum(running, jnp.max(masked, axis=-1))
    weights = jnp.where(allowed, jnp.exp(scores - newest[..., None]), 0.0)
    factor = jnp.exp(running - newest)
    denominator = denominator * factor + jnp.sum(weights, axis=-1)
    summed_output = summed_output * factor[..., None] + jnp.einsum(
        pattern, weights.astype(jnp.bfloat16), value_heads, preferred_element_type=jnp.float32
    )
    return (newest, denominator, summed_output)


def shards_general(
    x_prompt,
    x_suffix,
    norm_gain,
    w_query,
    w_key,
    w_value,
    query_gain,
    key_gain,
    adapter_down,
    adapter_up,
    prompt_len,
    member_count,
    suffix_len,
    adapter_id,
    holder_slot,
):
    fsdp_rank = lax.axis_index("fsdp")
    req_count = lax.axis_size("req")
    pr_rows = x_prompt.shape[1]
    mem_dev = x_suffix.shape[1]
    suf_rows = x_suffix.shape[2]
    model_width = x_prompt.shape[2]
    head_dim = query_gain.shape[0]
    q_cols = w_query.shape[1] * req_count
    kv_cols = w_key.shape[1] * req_count
    kv_heads = kv_cols // head_dim
    group_size = q_cols // kv_cols
    row_count = pr_rows + mem_dev * suf_rows
    prompt_total = prompt_len[0]
    tokens = jnp.concatenate(
        [x_prompt[0], x_suffix[0].reshape(mem_dev * suf_rows, model_width)], axis=0
    )
    normed = norm_rows(tokens.astype(jnp.float32), norm_gain).astype(jnp.bfloat16)
    full_q, full_k, full_v = (
        lax.all_gather(w_query, "req", axis=1, tiled=True),
        lax.all_gather(w_key, "req", axis=1, tiled=True),
        lax.all_gather(w_value, "req", axis=1, tiled=True),
    )
    pieces = (
        lax.all_gather(full_q, "fsdp", axis=0, tiled=True),
        lax.all_gather(full_k, "fsdp", axis=0, tiled=True),
        lax.all_gather(full_v, "fsdp", axis=0, tiled=True),
    )
    base_q, base_k, base_v = tuple(
        (
            jnp.dot(normed, weight_piece, preferred_element_type=jnp.float32)
            for weight_piece in pieces
        )
    )
    member_ids = adapter_id[0]
    store_rows = holder_slot.shape[0]
    lookup = jnp.where(
        member_ids[:, None] == jnp.arange(store_rows)[None, :], holder_slot[None, :], 0
    )
    storage = jnp.sum(lookup, axis=1)
    store_down, store_up = (
        lax.all_gather(adapter_down, "fsdp", axis=0, tiled=True),
        lax.all_gather(adapter_up, "fsdp", axis=0, tiled=True),
    )
    mine = lax.dynamic_slice_in_dim(storage, fsdp_rank * mem_dev, mem_dev)
    select_down_matrix = jnp.take(store_down, mine, axis=0)
    select_up_matrix = jnp.take(store_up, mine, axis=0)
    suffix_input_rows = normed[pr_rows:].reshape(mem_dev, suf_rows, model_width)
    reduced_rank_rows = jnp.einsum(
        "bve,bfe->bvf", suffix_input_rows, select_down_matrix, preferred_element_type=jnp.float32
    ).astype(jnp.bfloat16)
    adapter_delta = jnp.einsum(
        "wge,wet->wgt", reduced_rank_rows, select_up_matrix, preferred_element_type=jnp.float32
    )
    query_full = jnp.concatenate(
        [base_q[:pr_rows], base_q[pr_rows:] + adapter_delta.reshape(mem_dev * suf_rows, q_cols)],
        axis=0,
    )
    prompt_pos = fsdp_rank * pr_rows + jnp.arange(pr_rows)
    suffix_pos = prompt_total + jnp.tile(jnp.arange(suf_rows), mem_dev)
    positions = jnp.concatenate([prompt_pos, suffix_pos])
    queries = (
        shape_heads(query_full, query_gain, positions, head_dim)
        .astype(jnp.bfloat16)
        .reshape(row_count, kv_heads, group_size, head_dim)
    )
    key_heads = shape_heads(base_k, key_gain, positions, head_dim).astype(jnp.bfloat16)
    value_heads = base_v.astype(jnp.bfloat16).reshape(row_count, kv_heads, head_dim)
    limits = jnp.concatenate([prompt_pos, jnp.full((mem_dev * suf_rows,), 2**30, jnp.int32)])
    score_scale = head_dim ** (-0.5)
    start_state = (
        jnp.full((row_count, kv_heads, group_size), masked_low, jnp.float32),
        jnp.zeros((row_count, kv_heads, group_size), jnp.float32),
        jnp.zeros((row_count, kv_heads, group_size, head_dim), jnp.float32),
    )
    prompt_k_flat = key_heads[:pr_rows].reshape(pr_rows, kv_cols)
    prompt_v_flat = value_heads[:pr_rows].reshape(pr_rows, kv_cols)
    piece_keys = lax.all_gather(prompt_k_flat, "fsdp", axis=0, tiled=True)
    piece_values = lax.all_gather(prompt_v_flat, "fsdp", axis=0, tiled=True)
    piece_rows = piece_keys.shape[0]
    key_pos = jnp.arange(piece_rows)
    allowed = (key_pos[None, :] < prompt_total) & (key_pos[None, :] <= limits[:, None])
    scores = (
        jnp.einsum(
            "rkgd,nkd->rkgn",
            queries,
            piece_keys.reshape(piece_rows, kv_heads, head_dim),
            preferred_element_type=jnp.float32,
        )
        * score_scale
    )
    carried = update(
        start_state,
        scores,
        allowed[:, None, None, :],
        piece_values.reshape(piece_rows, kv_heads, head_dim),
        "rkgn,nkd->rkgd",
    )
    suffix_state = tuple(
        (
            state_part[pr_rows:].reshape((mem_dev, suf_rows) + state_part.shape[1:])
            for state_part in carried
        )
    )
    suffix_q = queries[pr_rows:].reshape(mem_dev, suf_rows, kv_heads, group_size, head_dim)
    suffix_k = key_heads[pr_rows:].reshape(mem_dev, suf_rows, kv_heads, head_dim)
    suffix_v = value_heads[pr_rows:].reshape(mem_dev, suf_rows, kv_heads, head_dim)
    own_scores = (
        jnp.einsum("mskgd,mtkd->mskgt", suffix_q, suffix_k, preferred_element_type=jnp.float32)
        * score_scale
    )
    causal = jnp.arange(suf_rows)[None, :] <= jnp.arange(suf_rows)[:, None]
    suffix_state = update(
        suffix_state, own_scores, causal[None, :, None, None, :], suffix_v, "mskgt,mtkd->mskgd"
    )
    denominator = jnp.concatenate(
        [carried[1][:pr_rows], suffix_state[1].reshape(mem_dev * suf_rows, kv_heads, group_size)],
        axis=0,
    )
    summed_output = jnp.concatenate(
        [
            carried[2][:pr_rows],
            suffix_state[2].reshape(mem_dev * suf_rows, kv_heads, group_size, head_dim),
        ],
        axis=0,
    )
    attended = (summed_output / denominator[..., None]).reshape(row_count, q_cols)
    member_index = fsdp_rank * mem_dev + jnp.arange(mem_dev)
    suffix_ok = (member_index < member_count[0])[:, None] & (
        jnp.arange(suf_rows)[None, :] < suffix_len[0][:, None]
    )
    valid_rows = jnp.concatenate([prompt_pos < prompt_total, suffix_ok.reshape(mem_dev * suf_rows)])
    result = jnp.where(valid_rows[:, None], attended, 0.0).astype(jnp.bfloat16)
    return (result[:pr_rows][None], result[pr_rows:].reshape(1, mem_dev, suf_rows, q_cols))


axes = ("fsdp", "req")
in_smem = pl.BlockSpec(memory_space=pltpu.SMEM)
in_vmem = pl.BlockSpec(memory_space=pltpu.VMEM)
in_hbm = pl.BlockSpec(memory_space=pltpu.HBM)
in_any = pl.BlockSpec(memory_space=pl.ANY)
nt_dims = (((1,), (1,)), ((), ()))
log2_e = 1.4426950408889634
head = 128


def device_number(x, y, z, core):
    return (y * 2 + x) * 8 + z * 2 + core


def pairs(target):
    return [
        (device_number(x, y, z, core), device_number(*target(x, y, z, core)))
        for y in range(2)
        for x in range(2)
        for z in range(4)
        for core in range(2)
    ]


first_hop = pairs(lambda x, y, z, c: (1 - x, y, z, c) if c == 0 else (x, 1 - y, z, c))
second_hop = pairs(lambda x, y, z, c: (x, 1 - y, z, c) if c == 0 else (1 - x, y, z, c))
ring_hop = pairs(lambda x, y, z, c: (x, y, (z + 1) % 4, c))
ring_back = pairs(lambda x, y, z, c: (x, y, (z + 3) % 4, c))
core_swap = pairs(lambda x, y, z, c: (x, y, z, 1 - c))


def permute(value, hop):
    return lax.ppermute(value, axes, hop)


def together(*values):
    return lax.optimization_barrier(values)


def slice_owners():
    rank = lax.axis_index("fsdp")
    core = lax.rem(lax.axis_index("req"), 2)
    x_side = rank + 1 - 2 * lax.rem(rank, 2)
    y_side = rank + 2 - 4 * (rank // 2)
    return (
        rank,
        (1 - core) * x_side + core * y_side,
        (1 - core) * y_side + core * x_side,
        3 - rank,
    )


def block_refs(refs):
    near, corner = refs[4:6]
    rows = corner.shape[0]
    theirs = tuple(near.at[part * rows : (part + 1) * rows, :] for part in range(3)) + (corner,)
    return tuple(refs[0:4]), theirs


def homes(steps):
    z = lax.axis_index("req") // 2
    return [lax.rem(z + 4 - step, 4) for step in steps]


def pack_kernel(
    key_ref, value_ref, query_ref, down_ref, up_ref, prompt_ref, own_ref, near_ref, buffers, sems
):
    core = lax.rem(lax.axis_index("req"), 2)
    half, depth = key_ref.shape
    rank = down_ref.shape[1]
    pr_rows, width = prompt_ref.shape
    query_buf, down_buf, up_buf = buffers
    tail = own_ref.shape[0] - pr_rows * (width // depth)
    copies = [
        pltpu.make_async_copy(query_ref, query_buf, sems.at[0]),
        pltpu.make_async_copy(down_ref, down_buf, sems.at[1]),
        pltpu.make_async_copy(up_ref, up_buf, sems.at[2]),
        pltpu.make_async_copy(key_ref, near_ref.at[pl.ds(0, half), :], sems.at[3]),
        pltpu.make_async_copy(value_ref, near_ref.at[pl.ds(half, half), :], sems.at[4]),
    ]
    for part in range(width // depth):
        copies.append(
            pltpu.make_async_copy(
                prompt_ref.at[:, pl.ds(part * depth, depth)],
                own_ref.at[pl.ds(tail + part * pr_rows, pr_rows), :],
                sems.at[5 + part],
            )
        )
    for copy in copies:
        copy.start()
    for copy in copies:
        copy.wait()
    near_ref[2 * half : 4 * half, :] = query_buf[...].T
    own_ref[0 : 4 * half, :] = near_ref[...]
    row = 4 * half
    for source in (down_buf, up_buf):
        for part in range(source.shape[2] // depth):
            own_ref[row : row + rank, :] = source[core, :, part * depth : (part + 1) * depth]
            row += rank


def norm_kernel(own_ref, side_ref, other_ref, corner_ref, suffix_ref, gain_ref, out_ref, *, tail):
    slices, _, depth = out_ref.shape
    width = slices * depth
    pr_rows = (own_ref.shape[0] - tail) // slices
    owners = slice_owners()
    row = 0
    for source in (side_ref, other_ref, corner_ref, own_ref):
        square = None
        for part in range(slices):
            start = tail + part * pr_rows
            values = source[start : start + pr_rows, :].astype(jnp.float32)
            added = jnp.sum(values * values, axis=-1, keepdims=True)
            square = added if square is None else square + added
        scale = lax.rsqrt(square * (1.0 / width) + epsilon)
        for index, owner in enumerate(owners):
            start = pl.multiple_of(tail + owner * pr_rows, 16)
            gain = gain_ref[:, pl.ds(pl.multiple_of(owner * depth, depth), depth)]
            values = source[pl.ds(start, pr_rows), :].astype(jnp.float32)
            out_ref[index, row : row + pr_rows, :] = (values * scale * gain).astype(jnp.bfloat16)
        row += pr_rows
    values = suffix_ref[...].astype(jnp.float32)
    scale = lax.rsqrt(jnp.mean(values * values, axis=-1, keepdims=True) + epsilon)
    for index, owner in enumerate(owners):
        at_slice = pl.ds(pl.multiple_of(owner * depth, depth), depth)
        part = suffix_ref[:, at_slice].astype(jnp.float32) * scale * gain_ref[:, at_slice]
        out_ref[index, row:, :] = part.astype(jnp.bfloat16)


def project(x_ref, rows, weight_blocks):
    total = None
    for index, block in enumerate(weight_blocks):
        part = lax.dot_general(
            x_ref[index, rows, :], block, nt_dims, preferred_element_type=jnp.float32
        )
        total = part if total is None else total + part
    return total


def adapter_kernel(x_ref, slot_ref, *refs, first_row):
    mine, theirs = block_refs(refs[:6])
    low_ref, up_ref = refs[6:]
    slices, _, depth = x_ref.shape
    rank_size = up_ref.shape[0] // 8
    owners = slice_owners()
    core = lax.rem(lax.axis_index("req"), 2)
    low = None
    for owner in range(slices):
        index = jnp.where(
            owner == owners[0],
            0,
            jnp.where(owner == owners[1], 1, jnp.where(owner == owners[2], 2, 3)),
        )
        row = 2 * head + owner * rank_size
        down = jnp.concatenate(
            [block[row : row + rank_size, :] for block in mine + theirs], axis=0
        )
        part = lax.dot_general(
            x_ref[index, first_row:, :], down, nt_dims, preferred_element_type=jnp.float32
        )
        low = part if low is None else low + part
    column = lax.broadcasted_iota(jnp.int32, low.shape, 1) // rank_size
    keep = jnp.zeros(low.shape, jnp.bool_)
    for side in range(2):
        parity = core if side == 0 else 1 - core
        for index, owner in enumerate(owners):
            held = owner * 2 + parity
            keep = keep | ((column == side * 4 + index) & (held == slot_ref[0]))
    low_ref[...] = jnp.where(keep, low, 0.0).astype(jnp.bfloat16)
    for part in range(up_ref.shape[1] // depth):
        row = 2 * head + (slices + part) * rank_size
        for index, block in enumerate(mine + theirs):
            up_ref[index * rank_size : (index + 1) * rank_size, part * depth : (part + 1) * depth] = (
                block[row : row + rank_size, :]
            )


def attend_kernel(*refs, steps, first):
    (info_ref, x_ref, cos_ref, sin_ref, q_gain_ref, k_gain_ref, low_ref, up_ref), refs = (
        refs[:8],
        refs[8:],
    )
    mine, theirs = block_refs(refs[:6])
    refs = refs[6:] if first else refs[8:]
    prompt_out, suffix_out, prompt_buf, suffix_buf, sems = refs
    pr_rows = prompt_buf.shape[0]
    suf_rows = suffix_buf.shape[0]
    prompt_keys = 4 * pr_rows
    first_query = prompt_keys - pr_rows
    count = len(steps)
    core = lax.rem(lax.axis_index("req"), 2)
    owners = slice_owners()
    rank = owners[0]

    def stacked(start):
        return [
            jnp.concatenate(
                [
                    block[step * 2 * head + start : step * 2 * head + start + head, :]
                    for block in (m, t)
                    for step in range(count)
                ],
                axis=0,
            )
            for m, t in zip(mine, theirs)
        ]

    kv_raw = project(x_ref, slice(None), stacked(0))
    q_raw = project(x_ref, slice(first_query, None), stacked(head))
    prompt_total = info_ref[0]
    member_ok = info_ref[1]
    suffix_total = info_ref[2]

    def key_positions(rows):
        column = lax.broadcasted_iota(jnp.int32, (rows, prompt_keys), 1)
        part = column // pr_rows
        owner = jnp.where(
            part == 0,
            owners[1],
            jnp.where(part == 1, owners[2], jnp.where(part == 2, owners[3], rank)),
        )
        return owner * pr_rows + column - part * pr_rows

    suffix_sees = jnp.where(key_positions(1) < prompt_total, 0.0, masked_low)
    row = lax.broadcasted_iota(jnp.int32, (pr_rows, prompt_keys), 0) + rank * pr_rows
    position = key_positions(pr_rows)
    prompt_sees = jnp.where((position < prompt_total) & (position <= row), 0.0, masked_low)
    prompt_sees = jnp.concatenate([prompt_sees, prompt_sees], axis=0)
    own_sees = jnp.where(
        lax.broadcasted_iota(jnp.int32, (suf_rows, suf_rows), 1)
        <= lax.broadcasted_iota(jnp.int32, (suf_rows, suf_rows), 0),
        0.0,
        masked_low,
    )
    prompt_ok = (
        lax.broadcasted_iota(jnp.int32, (pr_rows, 1), 0) + rank * pr_rows < prompt_total
    )
    suffix_ok = (lax.broadcasted_iota(jnp.int32, (suf_rows, 1), 0) < suffix_total) & (
        member_ok > 0
    )
    factor = head ** (-0.5) * log2_e
    half = head // 2
    cosine, minus_sine = cos_ref[:, 0:half], sin_ref[:, 0:half]
    q_cos, q_sin = cos_ref[first_query:, :], sin_ref[first_query:, :]
    low_gain, high_gain = k_gain_ref[:, 0:half], k_gain_ref[:, half:head]
    copies = []
    for index, home in enumerate(homes(steps)):
        own_part = kv_raw[:, index * head : (index + 1) * head]
        other_part = kv_raw[:, (count + index) * head : (count + index + 1) * head]
        lower = jnp.where(core == 0, own_part, other_part)
        upper = jnp.where(core == 0, other_part, own_part)
        low, high = lower[:, 0:half], upper[:, 0:half]
        square = jnp.sum(low * low + high * high, axis=-1, keepdims=True)
        scale = lax.rsqrt(square * (1.0 / head) + epsilon)
        low = low * scale * low_gain
        high = high * scale * high_gain
        keys = jnp.concatenate(
            [low * cosine + high * minus_sine, high * cosine - low * minus_sine], axis=-1
        ).astype(jnp.bfloat16)
        values = jnp.concatenate([lower[:, half:head], upper[:, half:head]], axis=-1)
        values = values.astype(jnp.bfloat16)
        queries = []
        for side in range(2):
            parity = core if side == 0 else 1 - core
            at_query = pl.ds(pl.multiple_of((2 * home + parity) * head, head), head)
            delta = jnp.dot(low_ref[...], up_ref[:, at_query], preferred_element_type=jnp.float32)
            place = (side * count + index) * head
            query = q_raw[:, place : place + head]
            query = jnp.concatenate([query[:pr_rows], query[pr_rows:] + delta], axis=0)
            scale = lax.rsqrt(jnp.mean(query * query, axis=-1, keepdims=True) + epsilon)
            query = query * scale * q_gain_ref[...]
            query = query * q_cos + pltpu.roll(query, half, 1) * q_sin
            queries.append(query.astype(jnp.bfloat16))
        scores = lax.dot_general(
            jnp.concatenate([query[:pr_rows] for query in queries], axis=0),
            keys[:prompt_keys],
            nt_dims,
            preferred_element_type=jnp.float32,
        )
        scores = scores * factor + prompt_sees
        weights = jnp.exp2(scores - jnp.max(scores, axis=-1, keepdims=True))
        total = jnp.sum(weights, axis=-1, keepdims=True)
        summed = jnp.dot(
            weights.astype(jnp.bfloat16), values[:prompt_keys], preferred_element_type=jnp.float32
        )
        summed = summed / total
        for side in range(2):
            parity = core if side == 0 else 1 - core
            at_side = pl.ds(pl.multiple_of((2 * index + parity) * head, head), head)
            prompt_buf[:, at_side] = jnp.where(
                prompt_ok, summed[side * pr_rows : (side + 1) * pr_rows], 0.0
            ).astype(jnp.bfloat16)
            scores = lax.dot_general(
                queries[side][pr_rows:], keys, nt_dims, preferred_element_type=jnp.float32
            )
            p_scores = scores[:, :prompt_keys] * factor + suffix_sees
            s_scores = scores[:, prompt_keys:] * factor + own_sees
            top = jnp.maximum(
                jnp.max(p_scores, axis=-1, keepdims=True),
                jnp.max(s_scores, axis=-1, keepdims=True),
            )
            weights = jnp.concatenate(
                [jnp.exp2(p_scores - top), jnp.exp2(s_scores - top)], axis=-1
            )
            total = jnp.sum(weights, axis=-1, keepdims=True)
            result = jnp.dot(
                weights.astype(jnp.bfloat16), values, preferred_element_type=jnp.float32
            )
            result = jnp.where(suffix_ok, result / total, 0.0)
            suffix_buf[:, at_side] = result.astype(jnp.bfloat16)
        at_pair = pl.ds(pl.multiple_of(home * 2 * head, 2 * head), 2 * head)
        for number, (buffer, out) in enumerate(((prompt_buf, prompt_out), (suffix_buf, suffix_out))):
            copy = pltpu.make_async_copy(
                buffer.at[:, pl.ds(index * 2 * head, 2 * head)],
                out.at[:, at_pair],
                sems.at[2 * index + number],
            )
            copy.start()
            copies.append(copy)
    for copy in copies:
        copy.wait()


def shards_torus(
    x_prompt,
    x_suffix,
    norm_gain,
    w_query,
    w_key,
    w_value,
    query_gain,
    key_gain,
    adapter_down,
    adapter_up,
    prompt_len,
    member_count,
    suffix_len,
    adapter_id,
    holder_slot,
):
    bf16 = jnp.bfloat16
    fsdp_rank = lax.axis_index("fsdp")
    pr_rows, model_width = x_prompt.shape[1:]
    suf_rows = x_suffix.shape[2]
    row_count = 4 * pr_rows + suf_rows
    depth = w_query.shape[0]
    slices = model_width // depth
    rank_size = adapter_down.shape[1]
    q_cols = adapter_up.shape[2]
    store_rows = (model_width + q_cols) // depth * rank_size
    tail = 2 * head + store_rows
    small = pltpu.CompilerParams(vmem_limit_bytes=12 << 20)

    def cost(flops, size):
        return pl.CostEstimate(flops=flops, bytes_accessed=size, transcendentals=0)

    own, near = pl.pallas_call(
        pack_kernel,
        out_shape=(
            jax.ShapeDtypeStruct((tail + slices * pr_rows, depth), bf16),
            jax.ShapeDtypeStruct((2 * head, depth), bf16),
        ),
        in_specs=[in_hbm] * 6,
        scratch_shapes=[
            (
                pltpu.VMEM(w_query.shape, bf16),
                pltpu.VMEM(adapter_down.shape, bf16),
                pltpu.VMEM(adapter_up.shape, bf16),
            ),
            pltpu.SemaphoreType.DMA((5 + slices,)),
        ],
        compiler_params=small,
        name="pack",
    )(
        *(
            pltpu.with_memory_space_constraint(operand, pltpu.HBM)
            for operand in (w_key.T, w_value.T, w_query, adapter_down, adapter_up, x_prompt[0])
        )
    )

    key_owners = slice_owners()
    prompt_pos = [owner * pr_rows + jnp.arange(pr_rows) for owner in key_owners]
    suffix_pos = prompt_len[0] + jnp.arange(suf_rows)
    positions = jnp.concatenate(prompt_pos[1:] + prompt_pos[:1] + [suffix_pos])
    half_dim = head // 2
    frequency = rope_base ** (-jnp.arange(half_dim).astype(jnp.float32) / half_dim)
    angles = positions.astype(jnp.float32)[:, None] * frequency[None, :]
    cosine, sine = jnp.cos(angles), jnp.sin(angles)
    cos_pair = jnp.concatenate([cosine, cosine], axis=1)
    sin_pair = jnp.concatenate([-sine, sine], axis=1)
    member = lax.dynamic_slice_in_dim(adapter_id[0], fsdp_rank, 1)
    slot = jnp.sum(
        jnp.where(member == jnp.arange(holder_slot.shape[0]), holder_slot, 0), keepdims=True
    )
    info = jnp.stack(
        [
            prompt_len[0],
            (fsdp_rank < member_count[0]).astype(jnp.int32),
            suffix_len[0, 0],
        ]
    )

    def swapped(*blocks, rows=None):
        return permute(jnp.concatenate([block[:rows] for block in blocks], axis=0), core_swap)

    own_side = permute(own, first_hop)
    own_other = permute(own, second_hop)
    step_one = permute(near, ring_hop)
    step_three = permute(near, ring_back)
    own, own_side, own_other, step_one, step_three, cos_pair, sin_pair, slot, info = together(
        own, own_side, own_other, step_one, step_three, cos_pair, sin_pair, slot, info
    )

    own_corner = permute(own_side, second_hop)
    along = permute(jnp.concatenate([step_one, own_side[: 2 * head]], axis=0), ring_hop)
    step_two, one_side = along[: 2 * head], along[2 * head :]
    three_side = permute(step_three, first_hop)
    far = jnp.concatenate([step_one, step_three], axis=0)
    far_other = permute(far, second_hop)
    own_near = swapped(own, own_other, own_side, rows=tail)
    own, own_side, own_other, own_corner, step_two, far, one_side, three_side, far_other, own_near = (
        together(
            own, own_side, own_other, own_corner, step_two,
            far, one_side, three_side, far_other, own_near,
        )
    )

    far_side = jnp.concatenate([one_side, three_side], axis=0)
    one_corner = permute(own_corner[: 2 * head], ring_hop)
    three_corner = permute(three_side, second_hop)
    two_side = permute(step_two, first_hop)
    two_other = permute(step_two, second_hop)
    own_blocks = (own, own_side, own_other, own_corner, own_near, swapped(own_corner, rows=tail))
    far_near = swapped(far, far_other, far_side)

    normed = pl.pallas_call(
        functools.partial(norm_kernel, tail=tail),
        out_shape=jax.ShapeDtypeStruct((slices, row_count, depth), bf16),
        compiler_params=small,
        cost_estimate=cost(0, row_count * model_width * 4),
        name="norm_rows",
    )(own, own_side, own_other, own_corner, x_suffix[0, 0], norm_gain[None, :])

    low, up = pl.pallas_call(
        functools.partial(adapter_kernel, first_row=4 * pr_rows),
        out_shape=(
            jax.ShapeDtypeStruct((suf_rows, 8 * rank_size), bf16),
            jax.ShapeDtypeStruct((8 * rank_size, q_cols), bf16),
        ),
        in_specs=[in_vmem, in_smem] + [in_vmem] * 6,
        compiler_params=small,
        cost_estimate=cost(2 * suf_rows * model_width * 8 * rank_size, 2 << 20),
        name="adapter",
    )(normed, slot, *own_blocks)

    def attend(steps, blocks, results):
        count = len(steps)
        return pl.pallas_call(
            functools.partial(attend_kernel, steps=steps, first=not results),
            out_shape=(
                jax.ShapeDtypeStruct((pr_rows, q_cols), bf16),
                jax.ShapeDtypeStruct((suf_rows, q_cols), bf16),
            ),
            in_specs=[in_smem] + [in_vmem] * 13 + [in_any] * len(results),
            out_specs=[in_any] * 2,
            scratch_shapes=[
                pltpu.VMEM((pr_rows, 2 * head * count), bf16),
                pltpu.VMEM((suf_rows, 2 * head * count), bf16),
                pltpu.SemaphoreType.DMA((2 * count,)),
            ],
            input_output_aliases={14: 0, 15: 1} if results else {},
            compiler_params=small,
            cost_estimate=cost(2 * row_count * model_width * 512 * count, count << 20),
            name="attend",
        )(
            info,
            normed,
            cos_pair,
            sin_pair,
            query_gain[None, :],
            key_gain[None, :],
            low,
            up,
            *blocks,
            *results,
        )

    results = attend((0,), own_blocks, ())
    one_corner, three_corner, step_two, two_side, two_other, far_near, *results = together(
        one_corner, three_corner, step_two, two_side, two_other, far_near, *results
    )
    far_corner = jnp.concatenate([one_corner, three_corner], axis=0)

    two_corner = permute(two_side, second_hop)
    far_blocks = (far, far_side, far_other, far_corner, far_near, swapped(far_corner))
    two_near = swapped(step_two, two_other, two_side)
    two_corner, two_near, *results = together(
        two_corner, two_near, *attend((1, 3), far_blocks, results)
    )
    two_blocks = (step_two, two_side, two_other, two_corner, two_near, swapped(two_corner))
    prompt_res, suffix_res = attend((2,), two_blocks, results)
    return prompt_res[None], suffix_res[None, None]


def shards(*operands):
    x_suffix, w_query, w_key, query_gain = operands[1], operands[3], operands[4], operands[6]
    head_dim = query_gain.shape[0]
    fits = (
        (lax.axis_size("fsdp"), lax.axis_size("req")) == (4, 8)
        and head_dim == 128
        and w_query.shape[1] == head_dim
        and 2 * w_key.shape[1] == head_dim
        and x_suffix.shape[1] == 1
        and operands[8].shape[0] == 2
    )
    return shards_torus(*operands) if fits else shards_general(*operands)


def solution(mesh):
    return jax.shard_map(
        shards,
        mesh=mesh,
        in_specs=(
            P("req", "fsdp", None),
            P("req", "fsdp", None, None),
            P(),
            P("fsdp", "req"),
            P("fsdp", "req"),
            P("fsdp", "req"),
            P(),
            P(),
            P("fsdp", None, None),
            P("fsdp", None, None),
            P("req"),
            P("req"),
            P("req", "fsdp"),
            P("req", None),
            P(),
        ),
        out_specs=(P("req", "fsdp", None), P("req", "fsdp", None, None)),
        check_vma=False,
    )
```

```python
import functools

import jax
import jax.numpy as jnp
from jax import lax
from jax.experimental import pallas as pl
from jax.experimental.pallas import tpu as pltpu
from jax.sharding import PartitionSpec as P

epsilon = 1e-06
rope_base = 1000000.0
masked_low = -1e30


def norm_rows(values, gain_vector):
    return (
        values
        * lax.rsqrt(jnp.mean(values * values, axis=-1, keepdims=True) + epsilon)
        * gain_vector
    )


def rotate(heads_in, positions):
    half_dim = heads_in.shape[-1] // 2
    frequency = rope_base ** (-jnp.arange(half_dim).astype(jnp.float32) / half_dim)
    angles = positions.astype(jnp.float32)[:, None] * frequency[None, :]
    cosine = jnp.cos(angles)[:, None, :]
    sine = jnp.sin(angles)[:, None, :]
    first_half = heads_in[..., :half_dim]
    second_half = heads_in[..., half_dim:]
    return jnp.concatenate(
        [first_half * cosine - second_half * sine, second_half * cosine + first_half * sine],
        axis=-1,
    )


def shape_heads(flat_rows, gain_vector, positions, head_dim):
    per_head = flat_rows.reshape(flat_rows.shape[0], flat_rows.shape[1] // head_dim, head_dim)
    return rotate(norm_rows(per_head, gain_vector), positions)


def update(carried, scores, allowed, value_heads, pattern):
    running, denominator, summed_output = carried
    masked = jnp.where(allowed, scores, masked_low)
    newest = jnp.maximum(running, jnp.max(masked, axis=-1))
    weights = jnp.where(allowed, jnp.exp(scores - newest[..., None]), 0.0)
    factor = jnp.exp(running - newest)
    denominator = denominator * factor + jnp.sum(weights, axis=-1)
    summed_output = summed_output * factor[..., None] + jnp.einsum(
        pattern, weights.astype(jnp.bfloat16), value_heads, preferred_element_type=jnp.float32
    )
    return (newest, denominator, summed_output)


def shards_general(
    x_prompt,
    x_suffix,
    norm_gain,
    w_query,
    w_key,
    w_value,
    query_gain,
    key_gain,
    adapter_down,
    adapter_up,
    prompt_len,
    member_count,
    suffix_len,
    adapter_id,
    holder_slot,
):
    fsdp_rank = lax.axis_index("fsdp")
    req_count = lax.axis_size("req")
    pr_rows = x_prompt.shape[1]
    mem_dev = x_suffix.shape[1]
    suf_rows = x_suffix.shape[2]
    model_width = x_prompt.shape[2]
    head_dim = query_gain.shape[0]
    q_cols = w_query.shape[1] * req_count
    kv_cols = w_key.shape[1] * req_count
    kv_heads = kv_cols // head_dim
    group_size = q_cols // kv_cols
    row_count = pr_rows + mem_dev * suf_rows
    prompt_total = prompt_len[0]
    tokens = jnp.concatenate(
        [x_prompt[0], x_suffix[0].reshape(mem_dev * suf_rows, model_width)], axis=0
    )
    normed = norm_rows(tokens.astype(jnp.float32), norm_gain).astype(jnp.bfloat16)
    full_q, full_k, full_v = (
        lax.all_gather(w_query, "req", axis=1, tiled=True),
        lax.all_gather(w_key, "req", axis=1, tiled=True),
        lax.all_gather(w_value, "req", axis=1, tiled=True),
    )
    pieces = (
        lax.all_gather(full_q, "fsdp", axis=0, tiled=True),
        lax.all_gather(full_k, "fsdp", axis=0, tiled=True),
        lax.all_gather(full_v, "fsdp", axis=0, tiled=True),
    )
    base_q, base_k, base_v = tuple(
        (
            jnp.dot(normed, weight_piece, preferred_element_type=jnp.float32)
            for weight_piece in pieces
        )
    )
    member_ids = adapter_id[0]
    store_rows = holder_slot.shape[0]
    lookup = jnp.where(
        member_ids[:, None] == jnp.arange(store_rows)[None, :], holder_slot[None, :], 0
    )
    storage = jnp.sum(lookup, axis=1)
    store_down, store_up = (
        lax.all_gather(adapter_down, "fsdp", axis=0, tiled=True),
        lax.all_gather(adapter_up, "fsdp", axis=0, tiled=True),
    )
    mine = lax.dynamic_slice_in_dim(storage, fsdp_rank * mem_dev, mem_dev)
    select_down_matrix = jnp.take(store_down, mine, axis=0)
    select_up_matrix = jnp.take(store_up, mine, axis=0)
    suffix_input_rows = normed[pr_rows:].reshape(mem_dev, suf_rows, model_width)
    reduced_rank_rows = jnp.einsum(
        "bve,bfe->bvf", suffix_input_rows, select_down_matrix, preferred_element_type=jnp.float32
    ).astype(jnp.bfloat16)
    adapter_delta = jnp.einsum(
        "wge,wet->wgt", reduced_rank_rows, select_up_matrix, preferred_element_type=jnp.float32
    )
    query_full = jnp.concatenate(
        [base_q[:pr_rows], base_q[pr_rows:] + adapter_delta.reshape(mem_dev * suf_rows, q_cols)],
        axis=0,
    )
    prompt_pos = fsdp_rank * pr_rows + jnp.arange(pr_rows)
    suffix_pos = prompt_total + jnp.tile(jnp.arange(suf_rows), mem_dev)
    positions = jnp.concatenate([prompt_pos, suffix_pos])
    queries = (
        shape_heads(query_full, query_gain, positions, head_dim)
        .astype(jnp.bfloat16)
        .reshape(row_count, kv_heads, group_size, head_dim)
    )
    key_heads = shape_heads(base_k, key_gain, positions, head_dim).astype(jnp.bfloat16)
    value_heads = base_v.astype(jnp.bfloat16).reshape(row_count, kv_heads, head_dim)
    limits = jnp.concatenate([prompt_pos, jnp.full((mem_dev * suf_rows,), 2**30, jnp.int32)])
    score_scale = head_dim ** (-0.5)
    start_state = (
        jnp.full((row_count, kv_heads, group_size), masked_low, jnp.float32),
        jnp.zeros((row_count, kv_heads, group_size), jnp.float32),
        jnp.zeros((row_count, kv_heads, group_size, head_dim), jnp.float32),
    )
    prompt_k_flat = key_heads[:pr_rows].reshape(pr_rows, kv_cols)
    prompt_v_flat = value_heads[:pr_rows].reshape(pr_rows, kv_cols)
    piece_keys = lax.all_gather(prompt_k_flat, "fsdp", axis=0, tiled=True)
    piece_values = lax.all_gather(prompt_v_flat, "fsdp", axis=0, tiled=True)
    piece_rows = piece_keys.shape[0]
    key_pos = jnp.arange(piece_rows)
    allowed = (key_pos[None, :] < prompt_total) & (key_pos[None, :] <= limits[:, None])
    scores = (
        jnp.einsum(
            "rkgd,nkd->rkgn",
            queries,
            piece_keys.reshape(piece_rows, kv_heads, head_dim),
            preferred_element_type=jnp.float32,
        )
        * score_scale
    )
    carried = update(
        start_state,
        scores,
        allowed[:, None, None, :],
        piece_values.reshape(piece_rows, kv_heads, head_dim),
        "rkgn,nkd->rkgd",
    )
    suffix_state = tuple(
        (
            state_part[pr_rows:].reshape((mem_dev, suf_rows) + state_part.shape[1:])
            for state_part in carried
        )
    )
    suffix_q = queries[pr_rows:].reshape(mem_dev, suf_rows, kv_heads, group_size, head_dim)
    suffix_k = key_heads[pr_rows:].reshape(mem_dev, suf_rows, kv_heads, head_dim)
    suffix_v = value_heads[pr_rows:].reshape(mem_dev, suf_rows, kv_heads, head_dim)
    own_scores = (
        jnp.einsum("mskgd,mtkd->mskgt", suffix_q, suffix_k, preferred_element_type=jnp.float32)
        * score_scale
    )
    causal = jnp.arange(suf_rows)[None, :] <= jnp.arange(suf_rows)[:, None]
    suffix_state = update(
        suffix_state, own_scores, causal[None, :, None, None, :], suffix_v, "mskgt,mtkd->mskgd"
    )
    denominator = jnp.concatenate(
        [carried[1][:pr_rows], suffix_state[1].reshape(mem_dev * suf_rows, kv_heads, group_size)],
        axis=0,
    )
    summed_output = jnp.concatenate(
        [
            carried[2][:pr_rows],
            suffix_state[2].reshape(mem_dev * suf_rows, kv_heads, group_size, head_dim),
        ],
        axis=0,
    )
    attended = (summed_output / denominator[..., None]).reshape(row_count, q_cols)
    member_index = fsdp_rank * mem_dev + jnp.arange(mem_dev)
    suffix_ok = (member_index < member_count[0])[:, None] & (
        jnp.arange(suf_rows)[None, :] < suffix_len[0][:, None]
    )
    valid_rows = jnp.concatenate([prompt_pos < prompt_total, suffix_ok.reshape(mem_dev * suf_rows)])
    result = jnp.where(valid_rows[:, None], attended, 0.0).astype(jnp.bfloat16)
    return (result[:pr_rows][None], result[pr_rows:].reshape(1, mem_dev, suf_rows, q_cols))


axes = ("fsdp", "req")
in_smem = pl.BlockSpec(memory_space=pltpu.SMEM)
in_vmem = pl.BlockSpec(memory_space=pltpu.VMEM)
in_hbm = pl.BlockSpec(memory_space=pltpu.HBM)
in_any = pl.BlockSpec(memory_space=pl.ANY)
nt_dims = (((1,), (1,)), ((), ()))
log2_e = 1.4426950408889634
head = 128


def device_number(x, y, z, core):
    return (y * 2 + x) * 8 + z * 2 + core


def pairs(target):
    return [
        (device_number(x, y, z, core), device_number(*target(x, y, z, core)))
        for y in range(2)
        for x in range(2)
        for z in range(4)
        for core in range(2)
    ]


first_hop = pairs(lambda x, y, z, c: (1 - x, y, z, c) if c == 0 else (x, 1 - y, z, c))
second_hop = pairs(lambda x, y, z, c: (x, 1 - y, z, c) if c == 0 else (1 - x, y, z, c))
ring_hop = pairs(lambda x, y, z, c: (x, y, (z + 1) % 4, c))
ring_back = pairs(lambda x, y, z, c: (x, y, (z + 3) % 4, c))
second_hop_across = pairs(
    lambda x, y, z, c: (x, 1 - y, z, 1 - c) if c == 0 else (1 - x, y, z, 1 - c)
)
core_swap = pairs(lambda x, y, z, c: (x, y, z, 1 - c))


def permute(value, hop):
    return lax.ppermute(value, axes, hop)


def together(*values):
    return lax.optimization_barrier(values)


def slice_owners():
    rank = lax.axis_index("fsdp")
    core = lax.rem(lax.axis_index("req"), 2)
    x_side = rank + 1 - 2 * lax.rem(rank, 2)
    y_side = rank + 2 - 4 * (rank // 2)
    return (
        rank,
        (1 - core) * x_side + core * y_side,
        (1 - core) * y_side + core * x_side,
        3 - rank,
    )


def block_refs(refs):
    near, corner = refs[4:6]
    rows = corner.shape[0]
    theirs = tuple(near.at[part * rows : (part + 1) * rows, :] for part in range(3)) + (corner,)
    return tuple(refs[0:4]), theirs


def homes(steps):
    z = lax.axis_index("req") // 2
    return [lax.rem(z + 4 - step, 4) for step in steps]


def pack_kernel(
    key_ref, value_ref, query_ref, down_ref, up_ref, prompt_ref, own_ref, near_ref, buffers, sems
):
    core = lax.rem(lax.axis_index("req"), 2)
    half, depth = key_ref.shape
    rank = down_ref.shape[1]
    pr_rows, width = prompt_ref.shape
    query_buf, down_buf, up_buf = buffers
    tail = own_ref.shape[0] - pr_rows * (width // depth)
    copies = [
        pltpu.make_async_copy(query_ref, query_buf, sems.at[0]),
        pltpu.make_async_copy(down_ref, down_buf, sems.at[1]),
        pltpu.make_async_copy(up_ref, up_buf, sems.at[2]),
        pltpu.make_async_copy(key_ref, near_ref.at[pl.ds(0, half), :], sems.at[3]),
        pltpu.make_async_copy(value_ref, near_ref.at[pl.ds(half, half), :], sems.at[4]),
    ]
    for part in range(width // depth):
        copies.append(
            pltpu.make_async_copy(
                prompt_ref.at[:, pl.ds(part * depth, depth)],
                own_ref.at[pl.ds(tail + part * pr_rows, pr_rows), :],
                sems.at[5 + part],
            )
        )
    for copy in copies:
        copy.start()
    for copy in copies:
        copy.wait()
    near_ref[2 * half : 4 * half, :] = query_buf[...].T
    own_ref[0 : 4 * half, :] = near_ref[...]
    row = 4 * half
    for source in (down_buf, up_buf):
        for part in range(source.shape[2] // depth):
            own_ref[row : row + rank, :] = source[core, :, part * depth : (part + 1) * depth]
            row += rank


def norm_kernel(own_ref, side_ref, other_ref, corner_ref, suffix_ref, gain_ref, out_ref, *, tail):
    slices, _, depth = out_ref.shape
    width = slices * depth
    pr_rows = (own_ref.shape[0] - tail) // slices
    owners = slice_owners()
    row = 0
    for source in (side_ref, other_ref, corner_ref, own_ref):
        square = None
        for part in range(slices):
            start = tail + part * pr_rows
            values = source[start : start + pr_rows, :].astype(jnp.float32)
            added = jnp.sum(values * values, axis=-1, keepdims=True)
            square = added if square is None else square + added
        scale = lax.rsqrt(square * (1.0 / width) + epsilon)
        for index, owner in enumerate(owners):
            start = pl.multiple_of(tail + owner * pr_rows, 16)
            gain = gain_ref[:, pl.ds(pl.multiple_of(owner * depth, depth), depth)]
            values = source[pl.ds(start, pr_rows), :].astype(jnp.float32)
            out_ref[index, row : row + pr_rows, :] = (values * scale * gain).astype(jnp.bfloat16)
        row += pr_rows
    values = suffix_ref[...].astype(jnp.float32)
    scale = lax.rsqrt(jnp.mean(values * values, axis=-1, keepdims=True) + epsilon)
    for index, owner in enumerate(owners):
        at_slice = pl.ds(pl.multiple_of(owner * depth, depth), depth)
        part = suffix_ref[:, at_slice].astype(jnp.float32) * scale * gain_ref[:, at_slice]
        out_ref[index, row:, :] = part.astype(jnp.bfloat16)


def project(x_ref, rows, weight_blocks):
    total = None
    for index, block in enumerate(weight_blocks):
        part = lax.dot_general(
            x_ref[index, rows, :], block, nt_dims, preferred_element_type=jnp.float32
        )
        total = part if total is None else total + part
    return total


def adapter_kernel(x_ref, slot_ref, *refs, first_row):
    mine, theirs = block_refs(refs[:6])
    low_ref, up_ref = refs[6:]
    slices, _, depth = x_ref.shape
    rank_size = up_ref.shape[0] // 8
    owners = slice_owners()
    core = lax.rem(lax.axis_index("req"), 2)
    low = None
    for owner in range(slices):
        index = jnp.where(
            owner == owners[0],
            0,
            jnp.where(owner == owners[1], 1, jnp.where(owner == owners[2], 2, 3)),
        )
        row = 2 * head + owner * rank_size
        down = jnp.concatenate(
            [block[row : row + rank_size, :] for block in mine + theirs], axis=0
        )
        part = lax.dot_general(
            x_ref[index, first_row:, :], down, nt_dims, preferred_element_type=jnp.float32
        )
        low = part if low is None else low + part
    column = lax.broadcasted_iota(jnp.int32, low.shape, 1) // rank_size
    keep = jnp.zeros(low.shape, jnp.bool_)
    for side in range(2):
        parity = core if side == 0 else 1 - core
        for index, owner in enumerate(owners):
            held = owner * 2 + parity
            keep = keep | ((column == side * 4 + index) & (held == slot_ref[0]))
    low_ref[...] = jnp.where(keep, low, 0.0).astype(jnp.bfloat16)
    for part in range(up_ref.shape[1] // depth):
        row = 2 * head + (slices + part) * rank_size
        for index, block in enumerate(mine + theirs):
            up_ref[index * rank_size : (index + 1) * rank_size, part * depth : (part + 1) * depth] = (
                block[row : row + rank_size, :]
            )


def attend_kernel(*refs, steps, first):
    (info_ref, x_ref, cos_ref, sin_ref, q_gain_ref, k_gain_ref, low_ref, up_ref), refs = (
        refs[:8],
        refs[8:],
    )
    mine, theirs = block_refs(refs[:6])
    refs = refs[6:] if first else refs[8:]
    prompt_out, suffix_out, prompt_buf, suffix_buf, sems = refs
    pr_rows = prompt_buf.shape[0]
    suf_rows = suffix_buf.shape[0]
    prompt_keys = 4 * pr_rows
    first_query = prompt_keys - pr_rows
    count = len(steps)
    core = lax.rem(lax.axis_index("req"), 2)
    owners = slice_owners()
    rank = owners[0]

    def stacked(start):
        return [
            jnp.concatenate(
                [
                    block[step * 2 * head + start : step * 2 * head + start + head, :]
                    for block in (m, t)
                    for step in range(count)
                ],
                axis=0,
            )
            for m, t in zip(mine, theirs)
        ]

    kv_raw = project(x_ref, slice(None), stacked(0))
    q_raw = project(x_ref, slice(first_query, None), stacked(head))
    prompt_total = info_ref[0:1, 0:1]
    member_ok = info_ref[1:2, 0:1]
    suffix_total = info_ref[2:3, 0:1]

    def key_positions(rows):
        column = lax.broadcasted_iota(jnp.int32, (rows, prompt_keys), 1)
        part = column // pr_rows
        owner = jnp.where(
            part == 0,
            owners[1],
            jnp.where(part == 1, owners[2], jnp.where(part == 2, owners[3], rank)),
        )
        return owner * pr_rows + column - part * pr_rows

    suffix_sees = jnp.where(key_positions(1) < prompt_total, 0.0, masked_low)
    row = lax.broadcasted_iota(jnp.int32, (pr_rows, prompt_keys), 0) + rank * pr_rows
    position = key_positions(pr_rows)
    prompt_sees = jnp.where((position < prompt_total) & (position <= row), 0.0, masked_low)
    prompt_sees = jnp.concatenate([prompt_sees, prompt_sees], axis=0)
    own_sees = jnp.where(
        lax.broadcasted_iota(jnp.int32, (suf_rows, suf_rows), 1)
        <= lax.broadcasted_iota(jnp.int32, (suf_rows, suf_rows), 0),
        0.0,
        masked_low,
    )
    prompt_ok = (
        lax.broadcasted_iota(jnp.int32, (pr_rows, 1), 0) + rank * pr_rows < prompt_total
    )
    suffix_ok = (lax.broadcasted_iota(jnp.int32, (suf_rows, 1), 0) < suffix_total) & (
        member_ok > 0
    )
    factor = head ** (-0.5) * log2_e
    half = head // 2
    cosine, minus_sine = cos_ref[:, 0:half], sin_ref[:, 0:half]
    q_cos, q_sin = cos_ref[first_query:, :], sin_ref[first_query:, :]
    low_gain, high_gain = k_gain_ref[:, 0:half], k_gain_ref[:, half:head]
    copies = []
    for index, home in enumerate(homes(steps)):
        own_part = kv_raw[:, index * head : (index + 1) * head]
        other_part = kv_raw[:, (count + index) * head : (count + index + 1) * head]
        lower = jnp.where(core == 0, own_part, other_part)
        upper = jnp.where(core == 0, other_part, own_part)
        low, high = lower[:, 0:half], upper[:, 0:half]
        square = jnp.sum(low * low + high * high, axis=-1, keepdims=True)
        scale = lax.rsqrt(square * (1.0 / head) + epsilon)
        low = low * scale * low_gain
        high = high * scale * high_gain
        keys = jnp.concatenate(
            [low * cosine + high * minus_sine, high * cosine - low * minus_sine], axis=-1
        ).astype(jnp.bfloat16)
        values = jnp.concatenate([lower[:, half:head], upper[:, half:head]], axis=-1)
        values = values.astype(jnp.bfloat16)
        queries = []
        for side in range(2):
            parity = core if side == 0 else 1 - core
            at_query = pl.ds(pl.multiple_of((2 * home + parity) * head, head), head)
            delta = jnp.dot(low_ref[...], up_ref[:, at_query], preferred_element_type=jnp.float32)
            place = (side * count + index) * head
            query = q_raw[:, place : place + head]
            query = jnp.concatenate([query[:pr_rows], query[pr_rows:] + delta], axis=0)
            scale = lax.rsqrt(jnp.mean(query * query, axis=-1, keepdims=True) + epsilon)
            query = query * scale * q_gain_ref[...]
            query = query * q_cos + pltpu.roll(query, half, 1) * q_sin
            queries.append(query.astype(jnp.bfloat16))
        scores = lax.dot_general(
            jnp.concatenate([query[:pr_rows] for query in queries], axis=0),
            keys[:prompt_keys],
            nt_dims,
            preferred_element_type=jnp.float32,
        )
        scores = scores * factor + prompt_sees
        weights = jnp.exp2(scores - jnp.max(scores, axis=-1, keepdims=True))
        total = jnp.sum(weights, axis=-1, keepdims=True)
        summed = jnp.dot(
            weights.astype(jnp.bfloat16), values[:prompt_keys], preferred_element_type=jnp.float32
        )
        summed = summed / total
        for side in range(2):
            parity = core if side == 0 else 1 - core
            at_side = pl.ds(pl.multiple_of((2 * index + parity) * head, head), head)
            prompt_buf[:, at_side] = jnp.where(
                prompt_ok, summed[side * pr_rows : (side + 1) * pr_rows], 0.0
            ).astype(jnp.bfloat16)
            scores = lax.dot_general(
                queries[side][pr_rows:], keys, nt_dims, preferred_element_type=jnp.float32
            )
            p_scores = scores[:, :prompt_keys] * factor + suffix_sees
            s_scores = scores[:, prompt_keys:] * factor + own_sees
            top = jnp.maximum(
                jnp.max(p_scores, axis=-1, keepdims=True),
                jnp.max(s_scores, axis=-1, keepdims=True),
            )
            weights = jnp.concatenate(
                [jnp.exp2(p_scores - top), jnp.exp2(s_scores - top)], axis=-1
            )
            total = jnp.sum(weights, axis=-1, keepdims=True)
            result = jnp.dot(
                weights.astype(jnp.bfloat16), values, preferred_element_type=jnp.float32
            )
            result = jnp.where(suffix_ok, result / total, 0.0)
            suffix_buf[:, at_side] = result.astype(jnp.bfloat16)
        at_pair = pl.ds(pl.multiple_of(home * 2 * head, 2 * head), 2 * head)
        for number, (buffer, out) in enumerate(((prompt_buf, prompt_out), (suffix_buf, suffix_out))):
            copy = pltpu.make_async_copy(
                buffer.at[:, pl.ds(index * 2 * head, 2 * head)],
                out.at[:, at_pair],
                sems.at[2 * index + number],
            )
            copy.start()
            copies.append(copy)
    for copy in copies:
        copy.wait()


def shards_torus(
    x_prompt,
    x_suffix,
    norm_gain,
    w_query,
    w_key,
    w_value,
    query_gain,
    key_gain,
    adapter_down,
    adapter_up,
    prompt_len,
    member_count,
    suffix_len,
    adapter_id,
    holder_slot,
):
    bf16 = jnp.bfloat16
    fsdp_rank = lax.axis_index("fsdp")
    pr_rows, model_width = x_prompt.shape[1:]
    suf_rows = x_suffix.shape[2]
    row_count = 4 * pr_rows + suf_rows
    depth = w_query.shape[0]
    slices = model_width // depth
    rank_size = adapter_down.shape[1]
    q_cols = adapter_up.shape[2]
    store_rows = (model_width + q_cols) // depth * rank_size
    tail = 2 * head + store_rows
    small = pltpu.CompilerParams(vmem_limit_bytes=12 << 20)

    def cost(flops, size):
        return pl.CostEstimate(flops=flops, bytes_accessed=size, transcendentals=0)

    own, near = pl.pallas_call(
        pack_kernel,
        out_shape=(
            jax.ShapeDtypeStruct((tail + slices * pr_rows, depth), bf16),
            jax.ShapeDtypeStruct((2 * head, depth), bf16),
        ),
        in_specs=[in_hbm] * 6,
        scratch_shapes=[
            (
                pltpu.VMEM(w_query.shape, bf16),
                pltpu.VMEM(adapter_down.shape, bf16),
                pltpu.VMEM(adapter_up.shape, bf16),
            ),
            pltpu.SemaphoreType.DMA((5 + slices,)),
        ],
        compiler_params=small,
        name="pack",
    )(
        *(
            pltpu.with_memory_space_constraint(operand, pltpu.HBM)
            for operand in (w_key.T, w_value.T, w_query, adapter_down, adapter_up, x_prompt[0])
        )
    )

    key_owners = slice_owners()
    prompt_pos = [owner * pr_rows + jnp.arange(pr_rows) for owner in key_owners]
    suffix_pos = prompt_len[0] + jnp.arange(suf_rows)
    positions = jnp.concatenate(prompt_pos[1:] + prompt_pos[:1] + [suffix_pos])
    half_dim = head // 2
    frequency = rope_base ** (-jnp.arange(half_dim).astype(jnp.float32) / half_dim)
    angles = positions.astype(jnp.float32)[:, None] * frequency[None, :]
    cosine, sine = jnp.cos(angles), jnp.sin(angles)
    cos_pair = jnp.concatenate([cosine, cosine], axis=1)
    sin_pair = jnp.concatenate([-sine, sine], axis=1)
    member = lax.dynamic_slice_in_dim(adapter_id[0], fsdp_rank, 1)
    slot = jnp.sum(
        jnp.where(member == jnp.arange(holder_slot.shape[0]), holder_slot, 0), keepdims=True
    )
    info = jnp.stack(
        [
            prompt_len[0],
            (fsdp_rank < member_count[0]).astype(jnp.int32),
            suffix_len[0, 0],
        ]
    )
    info = jnp.broadcast_to(info[:, None], (3, head))

    def swapped(*blocks, rows=None):
        return permute(jnp.concatenate([block[:rows] for block in blocks], axis=0), core_swap)

    own_side = permute(own, first_hop)
    own_other = permute(own, second_hop)
    step_one = permute(near, ring_hop)
    step_three = permute(near, ring_back)
    own, own_side, own_other, step_one, step_three, cos_pair, sin_pair, slot, info = together(
        own, own_side, own_other, step_one, step_three, cos_pair, sin_pair, slot, info
    )

    own_corner = permute(own_side, second_hop)
    along = permute(jnp.concatenate([step_one, own_side[: 2 * head]], axis=0), ring_hop)
    step_two, one_side = along[: 2 * head], along[2 * head :]
    three_side = permute(step_three, first_hop)
    far = jnp.concatenate([step_one, step_three], axis=0)
    far_other = permute(far, second_hop)
    own_near = swapped(own, own_other, own_side, rows=tail)
    own, own_side, own_other, own_corner, step_two, far, one_side, three_side, far_other, own_near = (
        together(
            own, own_side, own_other, own_corner, step_two,
            far, one_side, three_side, far_other, own_near,
        )
    )

    far_side = jnp.concatenate([one_side, three_side], axis=0)
    one_corner = permute(own_corner[: 2 * head], ring_hop)
    three_corner = permute(three_side, second_hop)
    two_side = permute(step_two, first_hop)
    two_other = permute(step_two, second_hop)
    own_blocks = (own, own_side, own_other, own_corner, own_near, swapped(own_corner, rows=tail))
    far_near = swapped(far, far_other, far_side)

    normed = pl.pallas_call(
        functools.partial(norm_kernel, tail=tail),
        out_shape=jax.ShapeDtypeStruct((slices, row_count, depth), bf16),
        compiler_params=small,
        cost_estimate=cost(0, row_count * model_width * 4),
        name="norm_rows",
    )(own, own_side, own_other, own_corner, x_suffix[0, 0], norm_gain[None, :])

    low, up = pl.pallas_call(
        functools.partial(adapter_kernel, first_row=4 * pr_rows),
        out_shape=(
            jax.ShapeDtypeStruct((suf_rows, 8 * rank_size), bf16),
            jax.ShapeDtypeStruct((8 * rank_size, q_cols), bf16),
        ),
        in_specs=[in_vmem, in_smem] + [in_vmem] * 6,
        compiler_params=small,
        cost_estimate=cost(2 * suf_rows * model_width * 8 * rank_size, 2 << 20),
        name="adapter",
    )(normed, slot, *own_blocks)

    def attend(steps, blocks, results):
        count = len(steps)
        return pl.pallas_call(
            functools.partial(attend_kernel, steps=steps, first=not results),
            out_shape=(
                jax.ShapeDtypeStruct((pr_rows, q_cols), bf16),
                jax.ShapeDtypeStruct((suf_rows, q_cols), bf16),
            ),
            in_specs=[in_vmem] * 14 + [in_any] * len(results),
            out_specs=[in_any] * 2,
            scratch_shapes=[
                pltpu.VMEM((pr_rows, 2 * head * count), bf16),
                pltpu.VMEM((suf_rows, 2 * head * count), bf16),
                pltpu.SemaphoreType.DMA((2 * count,)),
            ],
            input_output_aliases={14: 0, 15: 1} if results else {},
            compiler_params=small,
            cost_estimate=cost(2 * row_count * model_width * 512 * count, count << 20),
            name="attend",
        )(
            info,
            normed,
            cos_pair,
            sin_pair,
            query_gain[None, :],
            key_gain[None, :],
            low,
            up,
            *blocks,
            *results,
        )

    results = attend((0,), own_blocks, ())
    one_corner, three_corner, two_side, far_near, *results = together(
        one_corner, three_corner, two_side, far_near, *results
    )
    far_corner = jnp.concatenate([one_corner, three_corner], axis=0)

    two_corner = permute(two_side, second_hop)
    far_blocks = (far, far_side, far_other, far_corner, far_near, swapped(far_corner))
    two_near = swapped(step_two, two_other, two_side)
    two_across = permute(two_side, second_hop_across)
    two_corner, two_across, two_near, *results = together(
        two_corner, two_across, two_near, *attend((1, 3), far_blocks, results)
    )
    two_blocks = (step_two, two_side, two_other, two_corner, two_near, two_across)
    prompt_res, suffix_res = attend((2,), two_blocks, results)
    return prompt_res[None], suffix_res[None, None]


def shards(*operands):
    x_suffix, w_query, w_key, query_gain = operands[1], operands[3], operands[4], operands[6]
    head_dim = query_gain.shape[0]
    fits = (
        (lax.axis_size("fsdp"), lax.axis_size("req")) == (4, 8)
        and head_dim == 128
        and w_query.shape[1] == head_dim
        and 2 * w_key.shape[1] == head_dim
        and x_suffix.shape[1] == 1
        and operands[8].shape[0] == 2
    )
    return shards_torus(*operands) if fits else shards_general(*operands)


def solution(mesh):
    return jax.shard_map(
        shards,
        mesh=mesh,
        in_specs=(
            P("req", "fsdp", None),
            P("req", "fsdp", None, None),
            P(),
            P("fsdp", "req"),
            P("fsdp", "req"),
            P("fsdp", "req"),
            P(),
            P(),
            P("fsdp", None, None),
            P("fsdp", None, None),
            P("req"),
            P("req"),
            P("req", "fsdp"),
            P("req", None),
            P(),
        ),
        out_specs=(P("req", "fsdp", None), P("req", "fsdp", None, None)),
        check_vma=False,
    )
```

```python
import functools

import jax
import jax.numpy as jnp
from jax import lax
from jax.experimental import pallas as pl
from jax.experimental.pallas import tpu as pltpu
from jax.sharding import PartitionSpec as P

epsilon = 1e-06
rope_base = 1000000.0
masked_low = -1e30


def norm_rows(values, gain_vector):
    return (
        values
        * lax.rsqrt(jnp.mean(values * values, axis=-1, keepdims=True) + epsilon)
        * gain_vector
    )


def rotate(heads_in, positions):
    half_dim = heads_in.shape[-1] // 2
    frequency = rope_base ** (-jnp.arange(half_dim).astype(jnp.float32) / half_dim)
    angles = positions.astype(jnp.float32)[:, None] * frequency[None, :]
    cosine = jnp.cos(angles)[:, None, :]
    sine = jnp.sin(angles)[:, None, :]
    first_half = heads_in[..., :half_dim]
    second_half = heads_in[..., half_dim:]
    return jnp.concatenate(
        [first_half * cosine - second_half * sine, second_half * cosine + first_half * sine],
        axis=-1,
    )


def shape_heads(flat_rows, gain_vector, positions, head_dim):
    per_head = flat_rows.reshape(flat_rows.shape[0], flat_rows.shape[1] // head_dim, head_dim)
    return rotate(norm_rows(per_head, gain_vector), positions)


def update(carried, scores, allowed, value_heads, pattern):
    running, denominator, summed_output = carried
    masked = jnp.where(allowed, scores, masked_low)
    newest = jnp.maximum(running, jnp.max(masked, axis=-1))
    weights = jnp.where(allowed, jnp.exp(scores - newest[..., None]), 0.0)
    factor = jnp.exp(running - newest)
    denominator = denominator * factor + jnp.sum(weights, axis=-1)
    summed_output = summed_output * factor[..., None] + jnp.einsum(
        pattern, weights.astype(jnp.bfloat16), value_heads, preferred_element_type=jnp.float32
    )
    return (newest, denominator, summed_output)


def shards_general(
    x_prompt,
    x_suffix,
    norm_gain,
    w_query,
    w_key,
    w_value,
    query_gain,
    key_gain,
    adapter_down,
    adapter_up,
    prompt_len,
    member_count,
    suffix_len,
    adapter_id,
    holder_slot,
):
    fsdp_rank = lax.axis_index("fsdp")
    req_count = lax.axis_size("req")
    pr_rows = x_prompt.shape[1]
    mem_dev = x_suffix.shape[1]
    suf_rows = x_suffix.shape[2]
    model_width = x_prompt.shape[2]
    head_dim = query_gain.shape[0]
    q_cols = w_query.shape[1] * req_count
    kv_cols = w_key.shape[1] * req_count
    kv_heads = kv_cols // head_dim
    group_size = q_cols // kv_cols
    row_count = pr_rows + mem_dev * suf_rows
    prompt_total = prompt_len[0]
    tokens = jnp.concatenate(
        [x_prompt[0], x_suffix[0].reshape(mem_dev * suf_rows, model_width)], axis=0
    )
    normed = norm_rows(tokens.astype(jnp.float32), norm_gain).astype(jnp.bfloat16)
    full_q, full_k, full_v = (
        lax.all_gather(w_query, "req", axis=1, tiled=True),
        lax.all_gather(w_key, "req", axis=1, tiled=True),
        lax.all_gather(w_value, "req", axis=1, tiled=True),
    )
    pieces = (
        lax.all_gather(full_q, "fsdp", axis=0, tiled=True),
        lax.all_gather(full_k, "fsdp", axis=0, tiled=True),
        lax.all_gather(full_v, "fsdp", axis=0, tiled=True),
    )
    base_q, base_k, base_v = tuple(
        (
            jnp.dot(normed, weight_piece, preferred_element_type=jnp.float32)
            for weight_piece in pieces
        )
    )
    member_ids = adapter_id[0]
    store_rows = holder_slot.shape[0]
    lookup = jnp.where(
        member_ids[:, None] == jnp.arange(store_rows)[None, :], holder_slot[None, :], 0
    )
    storage = jnp.sum(lookup, axis=1)
    store_down, store_up = (
        lax.all_gather(adapter_down, "fsdp", axis=0, tiled=True),
        lax.all_gather(adapter_up, "fsdp", axis=0, tiled=True),
    )
    mine = lax.dynamic_slice_in_dim(storage, fsdp_rank * mem_dev, mem_dev)
    select_down_matrix = jnp.take(store_down, mine, axis=0)
    select_up_matrix = jnp.take(store_up, mine, axis=0)
    suffix_input_rows = normed[pr_rows:].reshape(mem_dev, suf_rows, model_width)
    reduced_rank_rows = jnp.einsum(
        "bve,bfe->bvf", suffix_input_rows, select_down_matrix, preferred_element_type=jnp.float32
    ).astype(jnp.bfloat16)
    adapter_delta = jnp.einsum(
        "wge,wet->wgt", reduced_rank_rows, select_up_matrix, preferred_element_type=jnp.float32
    )
    query_full = jnp.concatenate(
        [base_q[:pr_rows], base_q[pr_rows:] + adapter_delta.reshape(mem_dev * suf_rows, q_cols)],
        axis=0,
    )
    prompt_pos = fsdp_rank * pr_rows + jnp.arange(pr_rows)
    suffix_pos = prompt_total + jnp.tile(jnp.arange(suf_rows), mem_dev)
    positions = jnp.concatenate([prompt_pos, suffix_pos])
    queries = (
        shape_heads(query_full, query_gain, positions, head_dim)
        .astype(jnp.bfloat16)
        .reshape(row_count, kv_heads, group_size, head_dim)
    )
    key_heads = shape_heads(base_k, key_gain, positions, head_dim).astype(jnp.bfloat16)
    value_heads = base_v.astype(jnp.bfloat16).reshape(row_count, kv_heads, head_dim)
    limits = jnp.concatenate([prompt_pos, jnp.full((mem_dev * suf_rows,), 2**30, jnp.int32)])
    score_scale = head_dim ** (-0.5)
    start_state = (
        jnp.full((row_count, kv_heads, group_size), masked_low, jnp.float32),
        jnp.zeros((row_count, kv_heads, group_size), jnp.float32),
        jnp.zeros((row_count, kv_heads, group_size, head_dim), jnp.float32),
    )
    prompt_k_flat = key_heads[:pr_rows].reshape(pr_rows, kv_cols)
    prompt_v_flat = value_heads[:pr_rows].reshape(pr_rows, kv_cols)
    piece_keys = lax.all_gather(prompt_k_flat, "fsdp", axis=0, tiled=True)
    piece_values = lax.all_gather(prompt_v_flat, "fsdp", axis=0, tiled=True)
    piece_rows = piece_keys.shape[0]
    key_pos = jnp.arange(piece_rows)
    allowed = (key_pos[None, :] < prompt_total) & (key_pos[None, :] <= limits[:, None])
    scores = (
        jnp.einsum(
            "rkgd,nkd->rkgn",
            queries,
            piece_keys.reshape(piece_rows, kv_heads, head_dim),
            preferred_element_type=jnp.float32,
        )
        * score_scale
    )
    carried = update(
        start_state,
        scores,
        allowed[:, None, None, :],
        piece_values.reshape(piece_rows, kv_heads, head_dim),
        "rkgn,nkd->rkgd",
    )
    suffix_state = tuple(
        (
            state_part[pr_rows:].reshape((mem_dev, suf_rows) + state_part.shape[1:])
            for state_part in carried
        )
    )
    suffix_q = queries[pr_rows:].reshape(mem_dev, suf_rows, kv_heads, group_size, head_dim)
    suffix_k = key_heads[pr_rows:].reshape(mem_dev, suf_rows, kv_heads, head_dim)
    suffix_v = value_heads[pr_rows:].reshape(mem_dev, suf_rows, kv_heads, head_dim)
    own_scores = (
        jnp.einsum("mskgd,mtkd->mskgt", suffix_q, suffix_k, preferred_element_type=jnp.float32)
        * score_scale
    )
    causal = jnp.arange(suf_rows)[None, :] <= jnp.arange(suf_rows)[:, None]
    suffix_state = update(
        suffix_state, own_scores, causal[None, :, None, None, :], suffix_v, "mskgt,mtkd->mskgd"
    )
    denominator = jnp.concatenate(
        [carried[1][:pr_rows], suffix_state[1].reshape(mem_dev * suf_rows, kv_heads, group_size)],
        axis=0,
    )
    summed_output = jnp.concatenate(
        [
            carried[2][:pr_rows],
            suffix_state[2].reshape(mem_dev * suf_rows, kv_heads, group_size, head_dim),
        ],
        axis=0,
    )
    attended = (summed_output / denominator[..., None]).reshape(row_count, q_cols)
    member_index = fsdp_rank * mem_dev + jnp.arange(mem_dev)
    suffix_ok = (member_index < member_count[0])[:, None] & (
        jnp.arange(suf_rows)[None, :] < suffix_len[0][:, None]
    )
    valid_rows = jnp.concatenate([prompt_pos < prompt_total, suffix_ok.reshape(mem_dev * suf_rows)])
    result = jnp.where(valid_rows[:, None], attended, 0.0).astype(jnp.bfloat16)
    return (result[:pr_rows][None], result[pr_rows:].reshape(1, mem_dev, suf_rows, q_cols))


axes = ("fsdp", "req")
in_smem = pl.BlockSpec(memory_space=pltpu.SMEM)
in_vmem = pl.BlockSpec(memory_space=pltpu.VMEM)
in_hbm = pl.BlockSpec(memory_space=pltpu.HBM)
in_any = pl.BlockSpec(memory_space=pl.ANY)
nt_dims = (((1,), (1,)), ((), ()))
log2_e = 1.4426950408889634
head = 128


def device_number(x, y, z, core):
    return (y * 2 + x) * 8 + z * 2 + core


def pairs(target):
    return [
        (device_number(x, y, z, core), device_number(*target(x, y, z, core)))
        for y in range(2)
        for x in range(2)
        for z in range(4)
        for core in range(2)
    ]


first_hop = pairs(lambda x, y, z, c: (1 - x, y, z, c) if c == 0 else (x, 1 - y, z, c))
second_hop = pairs(lambda x, y, z, c: (x, 1 - y, z, c) if c == 0 else (1 - x, y, z, c))
ring_hop = pairs(lambda x, y, z, c: (x, y, (z + 1) % 4, c))
ring_back = pairs(lambda x, y, z, c: (x, y, (z + 3) % 4, c))
second_hop_across = pairs(
    lambda x, y, z, c: (x, 1 - y, z, 1 - c) if c == 0 else (1 - x, y, z, 1 - c)
)
core_swap = pairs(lambda x, y, z, c: (x, y, z, 1 - c))


def permute(value, hop):
    return lax.ppermute(value, axes, hop)


def together(*values):
    return lax.optimization_barrier(values)


def slice_owners():
    rank = lax.axis_index("fsdp")
    core = lax.rem(lax.axis_index("req"), 2)
    x_side = rank + 1 - 2 * lax.rem(rank, 2)
    y_side = rank + 2 - 4 * (rank // 2)
    return (
        rank,
        (1 - core) * x_side + core * y_side,
        (1 - core) * y_side + core * x_side,
        3 - rank,
    )


def block_refs(refs):
    near, corner = refs[4:6]
    rows = corner.shape[0]
    theirs = tuple(near.at[part * rows : (part + 1) * rows, :] for part in range(3)) + (corner,)
    return tuple(refs[0:4]), theirs


def homes(steps):
    z = lax.axis_index("req") // 2
    return [lax.rem(z + 4 - step, 4) for step in steps]


def pack_kernel(
    key_ref, value_ref, query_ref, down_ref, up_ref, prompt_ref, own_ref, near_ref, buffers, sems
):
    core = lax.rem(lax.axis_index("req"), 2)
    half, depth = key_ref.shape
    rank = down_ref.shape[1]
    pr_rows, width = prompt_ref.shape
    query_buf, down_buf, up_buf = buffers
    tail = own_ref.shape[0] - pr_rows * (width // depth)
    copies = [
        pltpu.make_async_copy(query_ref, query_buf, sems.at[0]),
        pltpu.make_async_copy(down_ref, down_buf, sems.at[1]),
        pltpu.make_async_copy(up_ref, up_buf, sems.at[2]),
        pltpu.make_async_copy(key_ref, near_ref.at[pl.ds(0, half), :], sems.at[3]),
        pltpu.make_async_copy(value_ref, near_ref.at[pl.ds(half, half), :], sems.at[4]),
    ]
    for part in range(width // depth):
        copies.append(
            pltpu.make_async_copy(
                prompt_ref.at[:, pl.ds(part * depth, depth)],
                own_ref.at[pl.ds(tail + part * pr_rows, pr_rows), :],
                sems.at[5 + part],
            )
        )
    for copy in copies:
        copy.start()
    for copy in copies:
        copy.wait()
    near_ref[2 * half : 4 * half, :] = query_buf[...].T
    own_ref[0 : 4 * half, :] = near_ref[...]
    row = 4 * half
    for source in (down_buf, up_buf):
        for part in range(source.shape[2] // depth):
            own_ref[row : row + rank, :] = source[core, :, part * depth : (part + 1) * depth]
            row += rank


def norm_kernel(own_ref, side_ref, other_ref, corner_ref, suffix_ref, gain_ref, out_ref, *, tail):
    slices, _, depth = out_ref.shape
    width = slices * depth
    pr_rows = (own_ref.shape[0] - tail) // slices
    owners = slice_owners()
    row = 0
    for source in (side_ref, other_ref, corner_ref, own_ref):
        square = None
        for part in range(slices):
            start = tail + part * pr_rows
            values = source[start : start + pr_rows, :].astype(jnp.float32)
            added = jnp.sum(values * values, axis=-1, keepdims=True)
            square = added if square is None else square + added
        scale = lax.rsqrt(square * (1.0 / width) + epsilon)
        for index, owner in enumerate(owners):
            start = pl.multiple_of(tail + owner * pr_rows, 16)
            gain = gain_ref[:, pl.ds(pl.multiple_of(owner * depth, depth), depth)]
            values = source[pl.ds(start, pr_rows), :].astype(jnp.float32)
            out_ref[index, row : row + pr_rows, :] = (values * scale * gain).astype(jnp.bfloat16)
        row += pr_rows
    values = suffix_ref[...].astype(jnp.float32)
    scale = lax.rsqrt(jnp.mean(values * values, axis=-1, keepdims=True) + epsilon)
    for index, owner in enumerate(owners):
        at_slice = pl.ds(pl.multiple_of(owner * depth, depth), depth)
        part = suffix_ref[:, at_slice].astype(jnp.float32) * scale * gain_ref[:, at_slice]
        out_ref[index, row:, :] = part.astype(jnp.bfloat16)


def project(x_ref, rows, weight_blocks):
    total = None
    for index, block in enumerate(weight_blocks):
        part = lax.dot_general(
            x_ref[index, rows, :], block, nt_dims, preferred_element_type=jnp.float32
        )
        total = part if total is None else total + part
    return total


def adapter_kernel(x_ref, slot_ref, *refs, first_row):
    mine, theirs = block_refs(refs[:6])
    low_ref, up_ref = refs[6:]
    slices, _, depth = x_ref.shape
    rank_size = up_ref.shape[0] // 8
    owners = slice_owners()
    core = lax.rem(lax.axis_index("req"), 2)
    low = None
    for owner in range(slices):
        index = jnp.where(
            owner == owners[0],
            0,
            jnp.where(owner == owners[1], 1, jnp.where(owner == owners[2], 2, 3)),
        )
        row = 2 * head + owner * rank_size
        down = jnp.concatenate(
            [block[row : row + rank_size, :] for block in mine + theirs], axis=0
        )
        part = lax.dot_general(
            x_ref[index, first_row:, :], down, nt_dims, preferred_element_type=jnp.float32
        )
        low = part if low is None else low + part
    column = lax.broadcasted_iota(jnp.int32, low.shape, 1) // rank_size
    keep = jnp.zeros(low.shape, jnp.bool_)
    for side in range(2):
        parity = core if side == 0 else 1 - core
        for index, owner in enumerate(owners):
            held = owner * 2 + parity
            keep = keep | ((column == side * 4 + index) & (held == slot_ref[0]))
    low_ref[...] = jnp.where(keep, low, 0.0).astype(jnp.bfloat16)
    for part in range(up_ref.shape[1] // depth):
        row = 2 * head + (slices + part) * rank_size
        for index, block in enumerate(mine + theirs):
            up_ref[index * rank_size : (index + 1) * rank_size, part * depth : (part + 1) * depth] = (
                block[row : row + rank_size, :]
            )


def attend_kernel(*refs, steps, first):
    (info_ref, x_ref, cos_ref, sin_ref, q_gain_ref, k_gain_ref, low_ref, up_ref), refs = (
        refs[:8],
        refs[8:],
    )
    mine, theirs = block_refs(refs[:6])
    refs = refs[6:] if first else refs[8:]
    prompt_out, suffix_out, prompt_buf, suffix_buf, sems = refs
    pr_rows = prompt_buf.shape[0]
    suf_rows = suffix_buf.shape[0]
    prompt_keys = 4 * pr_rows
    first_query = prompt_keys - pr_rows
    count = len(steps)
    core = lax.rem(lax.axis_index("req"), 2)
    owners = slice_owners()
    rank = owners[0]

    def stacked(start):
        return [
            jnp.concatenate(
                [
                    block[step * 2 * head + start : step * 2 * head + start + head, :]
                    for block in (m, t)
                    for step in range(count)
                ],
                axis=0,
            )
            for m, t in zip(mine, theirs)
        ]

    kv_raw = project(x_ref, slice(None), stacked(0))
    q_raw = project(x_ref, slice(first_query, None), stacked(head))
    prompt_total = info_ref[0:1, 0:1]
    member_ok = info_ref[1:2, 0:1]
    suffix_total = info_ref[2:3, 0:1]

    def key_positions(rows):
        column = lax.broadcasted_iota(jnp.int32, (rows, prompt_keys), 1)
        part = column // pr_rows
        owner = jnp.where(
            part == 0,
            owners[1],
            jnp.where(part == 1, owners[2], jnp.where(part == 2, owners[3], rank)),
        )
        return owner * pr_rows + column - part * pr_rows

    suffix_sees = jnp.where(key_positions(1) < prompt_total, 0.0, masked_low)
    row = lax.broadcasted_iota(jnp.int32, (pr_rows, prompt_keys), 0) + rank * pr_rows
    position = key_positions(pr_rows)
    prompt_sees = jnp.where((position < prompt_total) & (position <= row), 0.0, masked_low)
    prompt_sees = jnp.concatenate([prompt_sees, prompt_sees], axis=0)
    own_sees = jnp.where(
        lax.broadcasted_iota(jnp.int32, (suf_rows, suf_rows), 1)
        <= lax.broadcasted_iota(jnp.int32, (suf_rows, suf_rows), 0),
        0.0,
        masked_low,
    )
    prompt_ok = (
        lax.broadcasted_iota(jnp.int32, (pr_rows, 1), 0) + rank * pr_rows < prompt_total
    )
    suffix_ok = (lax.broadcasted_iota(jnp.int32, (suf_rows, 1), 0) < suffix_total) & (
        member_ok > 0
    )
    factor = head ** (-0.5) * log2_e
    half = head // 2
    cosine, minus_sine = cos_ref[:, 0:half], sin_ref[:, 0:half]
    q_cos, q_sin = cos_ref[first_query:, :], sin_ref[first_query:, :]
    low_gain, high_gain = k_gain_ref[:, 0:half], k_gain_ref[:, half:head]
    copies = []
    for index, home in enumerate(homes(steps)):
        own_part = kv_raw[:, index * head : (index + 1) * head]
        other_part = kv_raw[:, (count + index) * head : (count + index + 1) * head]
        lower = jnp.where(core == 0, own_part, other_part)
        upper = jnp.where(core == 0, other_part, own_part)
        low, high = lower[:, 0:half], upper[:, 0:half]
        square = jnp.sum(low * low + high * high, axis=-1, keepdims=True)
        scale = lax.rsqrt(square * (1.0 / head) + epsilon)
        low = low * scale * low_gain
        high = high * scale * high_gain
        keys = jnp.concatenate(
            [low * cosine + high * minus_sine, high * cosine - low * minus_sine], axis=-1
        ).astype(jnp.bfloat16)
        values = jnp.concatenate([lower[:, half:head], upper[:, half:head]], axis=-1)
        values = values.astype(jnp.bfloat16)
        queries = []
        for side in range(2):
            parity = core if side == 0 else 1 - core
            at_query = pl.ds(pl.multiple_of((2 * home + parity) * head, head), head)
            delta = jnp.dot(low_ref[...], up_ref[:, at_query], preferred_element_type=jnp.float32)
            place = (side * count + index) * head
            query = q_raw[:, place : place + head]
            query = jnp.concatenate([query[:pr_rows], query[pr_rows:] + delta], axis=0)
            scale = lax.rsqrt(jnp.mean(query * query, axis=-1, keepdims=True) + epsilon)
            query = query * scale * q_gain_ref[...]
            query = query * q_cos + pltpu.roll(query, half, 1) * q_sin
            queries.append(query.astype(jnp.bfloat16))
        scores = lax.dot_general(
            jnp.concatenate([query[:pr_rows] for query in queries], axis=0),
            keys[:prompt_keys],
            nt_dims,
            preferred_element_type=jnp.float32,
        )
        scores = scores * factor + prompt_sees
        weights = jnp.exp2(scores - jnp.max(scores, axis=-1, keepdims=True))
        total = jnp.sum(weights, axis=-1, keepdims=True)
        summed = jnp.dot(
            weights.astype(jnp.bfloat16), values[:prompt_keys], preferred_element_type=jnp.float32
        )
        summed = summed / total
        for side in range(2):
            parity = core if side == 0 else 1 - core
            at_side = pl.ds(pl.multiple_of((2 * index + parity) * head, head), head)
            prompt_buf[:, at_side] = jnp.where(
                prompt_ok, summed[side * pr_rows : (side + 1) * pr_rows], 0.0
            ).astype(jnp.bfloat16)
            scores = lax.dot_general(
                queries[side][pr_rows:], keys, nt_dims, preferred_element_type=jnp.float32
            )
            p_scores = scores[:, :prompt_keys] * factor + suffix_sees
            s_scores = scores[:, prompt_keys:] * factor + own_sees
            top = jnp.maximum(
                jnp.max(p_scores, axis=-1, keepdims=True),
                jnp.max(s_scores, axis=-1, keepdims=True),
            )
            weights = jnp.concatenate(
                [jnp.exp2(p_scores - top), jnp.exp2(s_scores - top)], axis=-1
            )
            total = jnp.sum(weights, axis=-1, keepdims=True)
            result = jnp.dot(
                weights.astype(jnp.bfloat16), values, preferred_element_type=jnp.float32
            )
            result = jnp.where(suffix_ok, result / total, 0.0)
            suffix_buf[:, at_side] = result.astype(jnp.bfloat16)
        at_pair = pl.ds(pl.multiple_of(home * 2 * head, 2 * head), 2 * head)
        for number, (buffer, out) in enumerate(((prompt_buf, prompt_out), (suffix_buf, suffix_out))):
            copy = pltpu.make_async_copy(
                buffer.at[:, pl.ds(index * 2 * head, 2 * head)],
                out.at[:, at_pair],
                sems.at[2 * index + number],
            )
            copy.start()
            copies.append(copy)
    for copy in copies:
        copy.wait()


def shards_torus(
    x_prompt,
    x_suffix,
    norm_gain,
    w_query,
    w_key,
    w_value,
    query_gain,
    key_gain,
    adapter_down,
    adapter_up,
    prompt_len,
    member_count,
    suffix_len,
    adapter_id,
    holder_slot,
):
    bf16 = jnp.bfloat16
    fsdp_rank = lax.axis_index("fsdp")
    pr_rows, model_width = x_prompt.shape[1:]
    suf_rows = x_suffix.shape[2]
    row_count = 4 * pr_rows + suf_rows
    depth = w_query.shape[0]
    slices = model_width // depth
    rank_size = adapter_down.shape[1]
    q_cols = adapter_up.shape[2]
    store_rows = (model_width + q_cols) // depth * rank_size
    tail = 2 * head + store_rows
    small = pltpu.CompilerParams(vmem_limit_bytes=12 << 20)

    def cost(flops, size):
        return pl.CostEstimate(flops=flops, bytes_accessed=size, transcendentals=0)

    own, near = pl.pallas_call(
        pack_kernel,
        out_shape=(
            jax.ShapeDtypeStruct((tail + slices * pr_rows, depth), bf16),
            jax.ShapeDtypeStruct((2 * head, depth), bf16),
        ),
        in_specs=[in_hbm] * 6,
        scratch_shapes=[
            (
                pltpu.VMEM(w_query.shape, bf16),
                pltpu.VMEM(adapter_down.shape, bf16),
                pltpu.VMEM(adapter_up.shape, bf16),
            ),
            pltpu.SemaphoreType.DMA((5 + slices,)),
        ],
        compiler_params=small,
        name="pack",
    )(
        *(
            pltpu.with_memory_space_constraint(operand, pltpu.HBM)
            for operand in (w_key.T, w_value.T, w_query, adapter_down, adapter_up, x_prompt[0])
        )
    )

    key_owners = slice_owners()
    prompt_pos = [owner * pr_rows + jnp.arange(pr_rows) for owner in key_owners]
    suffix_pos = prompt_len[0] + jnp.arange(suf_rows)
    positions = jnp.concatenate(prompt_pos[1:] + prompt_pos[:1] + [suffix_pos])
    half_dim = head // 2
    frequency = rope_base ** (-jnp.arange(half_dim).astype(jnp.float32) / half_dim)
    angles = positions.astype(jnp.float32)[:, None] * frequency[None, :]
    cosine, sine = jnp.cos(angles), jnp.sin(angles)
    cos_pair = jnp.concatenate([cosine, cosine], axis=1)
    sin_pair = jnp.concatenate([-sine, sine], axis=1)
    member = lax.dynamic_slice_in_dim(adapter_id[0], fsdp_rank, 1)
    slot = jnp.sum(
        jnp.where(member == jnp.arange(holder_slot.shape[0]), holder_slot, 0), keepdims=True
    )
    info = jnp.stack(
        [
            prompt_len[0],
            (fsdp_rank < member_count[0]).astype(jnp.int32),
            suffix_len[0, 0],
        ]
    )
    info = jnp.broadcast_to(info[:, None], (3, head))

    def swapped(*blocks, rows=None):
        return permute(jnp.concatenate([block[:rows] for block in blocks], axis=0), core_swap)

    own_side = permute(own, first_hop)
    own_other = permute(own, second_hop)
    step_one = permute(near, ring_hop)
    step_three = permute(near, ring_back)
    own, own_side, own_other, step_one, step_three, cos_pair, sin_pair, slot, info = together(
        own, own_side, own_other, step_one, step_three, cos_pair, sin_pair, slot, info
    )

    own_corner = permute(own_side, second_hop)
    step_two = permute(step_one, ring_hop)
    one_side = permute(own_side[: 2 * head], ring_hop)
    three_side = permute(step_three, first_hop)
    far = jnp.concatenate([step_one, step_three], axis=0)
    far_other = permute(far, second_hop)
    own_near = swapped(own, own_other, own_side, rows=tail)
    own, own_side, own_other, own_corner, step_two, far, one_side, three_side, far_other, own_near = (
        together(
            own, own_side, own_other, own_corner, step_two,
            far, one_side, three_side, far_other, own_near,
        )
    )

    far_side = jnp.concatenate([one_side, three_side], axis=0)
    one_corner = permute(own_corner[: 2 * head], ring_hop)
    three_corner = permute(three_side, second_hop)
    two_side = permute(step_two, first_hop)
    two_other = permute(step_two, second_hop)
    own_blocks = (own, own_side, own_other, own_corner, own_near, swapped(own_corner, rows=tail))
    far_near = swapped(far, far_other, far_side)

    normed = pl.pallas_call(
        functools.partial(norm_kernel, tail=tail),
        out_shape=jax.ShapeDtypeStruct((slices, row_count, depth), bf16),
        compiler_params=small,
        cost_estimate=cost(0, row_count * model_width * 4),
        name="norm_rows",
    )(own, own_side, own_other, own_corner, x_suffix[0, 0], norm_gain[None, :])

    low, up = pl.pallas_call(
        functools.partial(adapter_kernel, first_row=4 * pr_rows),
        out_shape=(
            jax.ShapeDtypeStruct((suf_rows, 8 * rank_size), bf16),
            jax.ShapeDtypeStruct((8 * rank_size, q_cols), bf16),
        ),
        in_specs=[in_vmem, in_smem] + [in_vmem] * 6,
        compiler_params=small,
        cost_estimate=cost(2 * suf_rows * model_width * 8 * rank_size, 2 << 20),
        name="adapter",
    )(normed, slot, *own_blocks)

    def attend(steps, blocks, results):
        count = len(steps)
        return pl.pallas_call(
            functools.partial(attend_kernel, steps=steps, first=not results),
            out_shape=(
                jax.ShapeDtypeStruct((pr_rows, q_cols), bf16),
                jax.ShapeDtypeStruct((suf_rows, q_cols), bf16),
            ),
            in_specs=[in_vmem] * 14 + [in_any] * len(results),
            out_specs=[in_any] * 2,
            scratch_shapes=[
                pltpu.VMEM((pr_rows, 2 * head * count), bf16),
                pltpu.VMEM((suf_rows, 2 * head * count), bf16),
                pltpu.SemaphoreType.DMA((2 * count,)),
            ],
            input_output_aliases={14: 0, 15: 1} if results else {},
            compiler_params=small,
            cost_estimate=cost(2 * row_count * model_width * 512 * count, count << 20),
            name="attend",
        )(
            info,
            normed,
            cos_pair,
            sin_pair,
            query_gain[None, :],
            key_gain[None, :],
            low,
            up,
            *blocks,
            *results,
        )

    results = attend((0,), own_blocks, ())
    one_corner, three_corner, two_side, far_near, *results = together(
        one_corner, three_corner, two_side, far_near, *results
    )
    far_corner = jnp.concatenate([one_corner, three_corner], axis=0)

    two_corner = permute(two_side, second_hop)
    far_blocks = (far, far_side, far_other, far_corner, far_near, swapped(far_corner))
    two_near = swapped(step_two, two_other, two_side)
    two_across = permute(two_side, second_hop_across)
    two_corner, two_across, two_near, *results = together(
        two_corner, two_across, two_near, *attend((1, 3), far_blocks, results)
    )
    two_blocks = (step_two, two_side, two_other, two_corner, two_near, two_across)
    prompt_res, suffix_res = attend((2,), two_blocks, results)
    return prompt_res[None], suffix_res[None, None]


def shards(*operands):
    x_suffix, w_query, w_key, query_gain = operands[1], operands[3], operands[4], operands[6]
    head_dim = query_gain.shape[0]
    fits = (
        (lax.axis_size("fsdp"), lax.axis_size("req")) == (4, 8)
        and head_dim == 128
        and w_query.shape[1] == head_dim
        and 2 * w_key.shape[1] == head_dim
        and x_suffix.shape[1] == 1
        and operands[8].shape[0] == 2
    )
    return shards_torus(*operands) if fits else shards_general(*operands)


def solution(mesh):
    return jax.shard_map(
        shards,
        mesh=mesh,
        in_specs=(
            P("req", "fsdp", None),
            P("req", "fsdp", None, None),
            P(),
            P("fsdp", "req"),
            P("fsdp", "req"),
            P("fsdp", "req"),
            P(),
            P(),
            P("fsdp", None, None),
            P("fsdp", None, None),
            P("req"),
            P("req"),
            P("req", "fsdp"),
            P("req", None),
            P(),
        ),
        out_specs=(P("req", "fsdp", None), P("req", "fsdp", None, None)),
        check_vma=False,
    )
```
